32 devices in a mesh: horiz: 8 (over z, y), depth: 4 (over x, core).
Axes of the slice: x: 2, y: 2, z: 4, core: 2. Of those that a mesh axis runs over, the one named last changes fastest.
Arguments:
- adjoint_state: float32 [9, 32, 128, 128], P(None, 'depth', 'horiz'), may hold values from -6 to 6
- buoyancy: float32 [32, 128, 128], P('depth', 'horiz'), may hold values from 0.5 to 1
- lame_lambda: float32 [32, 128, 128], P('depth', 'horiz'), may hold values from 0.5 to 1.5
- shear_modulus: float32 [32, 128, 128], P('depth', 'horiz'), may hold values from 0.3 to 1
- forward_field: float32 [32, 128, 128], P('depth', 'horiz'), may hold values from -6 to 6
- traces: float32 [256, 32, 128], P('horiz', 'depth'), may hold values from -6 to 6
- observed: float32 [4, 2, 512, 256], P('depth', None, 'horiz'), may hold values from -6 to 6
- pairs: int32 [256, 2], replicated, may hold values from 0 to 255
- patch_basis: float32 [16, 128], P(None, 'horiz'), may hold values from -0.375 to 0.375
- patch_ids: int32 [8, 16], P('horiz'), may hold values from 0 to 31, as said below
- slot_counts: int32 [8], P('horiz'), may hold values from 8 to 16, as said below
- owner_map: int32 [32], replicated, may hold values from 0 to 7, as said below
Outputs:
- adjoint_final: float32 [9, 32, 128, 128], P(None, 'depth', 'horiz')
- cross_spectra: float32 [4, 2, 512, 256], P('depth', None, 'horiz')
- patch_grad: float32 [4, 64, 128], P('depth', 'horiz')
The draws below stay inside these ranges and needn't reach their ends.
Inputs may be any that keep to these rules, and one draw needn't show every extreme that they name: Tile h uses its first slot_counts[h] slots; some tile uses all 16. `patch_ids`: the patches named in one tile are distinct; among the used slots of one tile at most 2 name patches of one owner, and some tile reaches 2. `owner_map`: every owner holds 2 or more patches and at most 8; some owner holds exactly 8.
All inputs are finite; a program needn't handle non-finite values.
Results may differ from the reference program's by a relative error of at most 0.00012.
Values sent between devices are 32-bit elements; how exact they have to be, the bound alone decides.
A program may use at most 64 MiB of HBM per device.

```python
import math
import jax
import jax.numpy as jnp
from jax import lax

CX = 16
CY = 128
LEVELS = 32
CZ = 8
NX = 128
ITERS = 4
S_DEV = 32
NT = 128
NF = 64
BLK_DEV = 8
TILES = 8
SLABS = 4
GROUPS = 4
STATIONS = 256
PAIRS = 256
GITEMS = 512
ITEMS = 2048
SLOTS = 16
NPATCH = 32
OWN_CAP = 8


def patch_plan(key):
    base = jax.random.fold_in(key, 9137)
    keys = jax.random.split(base, 7)
    owner_order = jax.random.permutation(keys[0], TILES)
    pattern = jnp.array([OWN_CAP, OWN_CAP // 2, 2, 2], jnp.int32)
    rank_counts = pattern[jnp.arange(TILES) % 4]
    owner_counts = jnp.zeros((TILES,), jnp.int32).at[owner_order].set(rank_counts)
    owner_start = jnp.cumsum(owner_counts) - owner_counts
    owner_sorted = jnp.repeat(jnp.arange(TILES, dtype=jnp.int32), owner_counts, total_repeat_length=NPATCH)
    shuffle = jax.random.permutation(keys[1], NPATCH).astype(jnp.int32)
    owner_table = jnp.zeros((NPATCH,), jnp.int32).at[shuffle].set(owner_sorted)
    first_pick = jax.random.randint(keys[2], (TILES, TILES), 0, owner_counts[None, :])
    second_pick = (first_pick + 1 + jax.random.randint(keys[3], (TILES, TILES), 0, owner_counts[None, :] - 1)) % owner_counts[None, :]
    first_ids = shuffle[owner_start[None, :] + first_pick]
    second_ids = shuffle[owner_start[None, :] + second_pick]
    listed = jnp.stack([first_ids, second_ids], axis=2).reshape(TILES, SLOTS)
    row_keys = jax.random.split(keys[4], TILES)

    def row_order(row_key):
        return jax.random.permutation(row_key, SLOTS)
    orders = jax.vmap(row_order)(row_keys)
    listed = jnp.take_along_axis(listed, orders, axis=1).astype(jnp.int32)
    counts = jax.random.randint(keys[5], (TILES,), SLOTS // 2, SLOTS + 1)
    full_tile = jax.random.randint(keys[6], (), 0, TILES)
    counts = counts.at[full_tile].set(SLOTS).astype(jnp.int32)
    return (listed, counts, owner_table)


def draw_patch_ids(key, part):
    return patch_plan(key)[0]


def draw_slot_counts(key, part):
    return patch_plan(key)[1]


def draw_owner_map(key, part):
    return patch_plan(key)[2]


def with_ends(entries, rng, smallest, top_value):
    place = [jax.random.randint(jax.random.fold_in(rng, axis), (), 0, length) for axis, length in enumerate(entries.shape)]
    widest = entries.shape.index(max(entries.shape))
    next_to = place[:widest] + [(place[widest] + 1) % entries.shape[widest]] + place[widest + 1:]
    return entries.at[tuple(place)].set(smallest).at[tuple(next_to)].set(top_value)


def level_of(stream_key, shape, shards, smallest, high):
    loudness, own = 1.0, jax.random.fold_in(stream_key, 6)
    for position, shards_of in shards:
        heights = jnp.exp(jax.random.uniform(jax.random.fold_in(own, position), (shards_of,), jnp.float32, smallest / len(shards), high / len(shards)))
        loudness = loudness * jnp.repeat(heights, shape[position] // shards_of).reshape([-1 if axis == position else 1 for axis in range(len(shape))])
    return loudness


def bell_draw(own_key, shape, spread, reach, cuts=(), held_as=jnp.bfloat16):
    result = spread * jax.random.normal(own_key, shape, jnp.float32)
    if cuts:
        result = result * level_of(own_key, shape, cuts, -0.22, 0.18)
    return jnp.clip(result, -reach, reach).astype(held_as)


def setup_inputs(seed: int = 0) -> dict:
    arg_keys = jax.random.split(jax.random.key(seed), 13)
    return {
        "adjoint_state": bell_draw(arg_keys[0], (9, LEVELS, NX, CY), 1.0, 6.0, ((1, 4), (2, 8)), jnp.float32),
        "buoyancy": jnp.clip(0.5 + 0.5 * jax.random.uniform(arg_keys[1], (LEVELS, NX, CY), jnp.float32) ** level_of(arg_keys[1], (LEVELS, NX, CY), ((0, 4), (1, 8)), -0.2, 0.2), 0.5, 1.0),
        "lame_lambda": jnp.clip(0.5 + 1.0 * jax.random.uniform(arg_keys[2], (LEVELS, NX, CY), jnp.float32) ** level_of(arg_keys[2], (LEVELS, NX, CY), ((0, 4), (1, 8)), -0.2, 0.2), 0.5, 1.5),
        "shear_modulus": jnp.clip(0.3 + 0.7 * jax.random.uniform(arg_keys[3], (LEVELS, NX, CY), jnp.float32) ** level_of(arg_keys[3], (LEVELS, NX, CY), ((0, 4), (1, 8)), -0.2, 0.2), 0.3, 1.0),
        "forward_field": bell_draw(arg_keys[4], (LEVELS, NX, CY), 1.0, 6.0, ((0, 4), (1, 8)), jnp.float32),
        "traces": bell_draw(arg_keys[5], (STATIONS, BLK_DEV * GROUPS, NT), 1.0, 6.0, ((0, 8), (1, 4)), jnp.float32),
        "observed": bell_draw(arg_keys[6], (GROUPS, 2, GITEMS, PAIRS), 1.0, 6.0, ((0, 4), (2, 8)), jnp.float32),
        "pairs": with_ends(jax.random.randint(arg_keys[7], (PAIRS, 2), 0, STATIONS), jax.random.fold_in(arg_keys[7], 1), 0, STATIONS - 1).astype(jnp.int32),
        "patch_basis": bell_draw(arg_keys[8], (SLOTS, NX), (2 * CX * TILES) ** -0.5, 0.375, ((1, 8),), jnp.float32),
        "patch_ids": draw_patch_ids(jax.random.fold_in(arg_keys[12], 71), 0),
        "slot_counts": draw_slot_counts(jax.random.fold_in(arg_keys[12], 71), 0),
        "owner_map": draw_owner_map(jax.random.fold_in(arg_keys[12], 71), 0),
    }


time_step = 0.25
precise_mode = lax.Precision.HIGHEST

def forward_diff(field, along):
    extent = field.shape[along]
    ahead = jnp.concatenate([lax.slice_in_dim(field, 1, extent, axis=along), jnp.zeros_like(lax.slice_in_dim(field, 0, 1, axis=along))], axis=along)
    return ahead - field

def backward_diff(field, along):
    extent = field.shape[along]
    behind = jnp.concatenate([jnp.zeros_like(lax.slice_in_dim(field, 0, 1, axis=along)), lax.slice_in_dim(field, 0, extent - 1, axis=along)], axis=along)
    return field - behind

def leapfrog(fields, buoyancy, lame_lambda, shear_modulus):
    vel_x, vel_y, vel_z, str_xx, str_yy, str_zz, str_xy, str_xz, str_yz = fields
    vel_x = vel_x + time_step * buoyancy * (forward_diff(str_xx, 1) + backward_diff(str_xy, 2) + backward_diff(str_xz, 0))
    vel_y = vel_y + time_step * buoyancy * (backward_diff(str_xy, 1) + forward_diff(str_yy, 2) + backward_diff(str_yz, 0))
    vel_z = vel_z + time_step * buoyancy * (backward_diff(str_xz, 1) + backward_diff(str_yz, 2) + forward_diff(str_zz, 0))
    strain_xx = backward_diff(vel_x, 1)
    strain_yy = backward_diff(vel_y, 2)
    strain_zz = backward_diff(vel_z, 0)
    p_modulus = lame_lambda + 2.0 * shear_modulus
    str_xx = str_xx + time_step * (p_modulus * strain_xx + lame_lambda * (strain_yy + strain_zz))
    str_yy = str_yy + time_step * (p_modulus * strain_yy + lame_lambda * (strain_xx + strain_zz))
    str_zz = str_zz + time_step * (p_modulus * strain_zz + lame_lambda * (strain_xx + strain_yy))
    str_xy = str_xy + time_step * shear_modulus * (forward_diff(vel_x, 2) + forward_diff(vel_y, 1))
    str_xz = str_xz + time_step * shear_modulus * (forward_diff(vel_x, 0) + forward_diff(vel_z, 1))
    str_yz = str_yz + time_step * shear_modulus * (forward_diff(vel_y, 0) + forward_diff(vel_z, 2))
    return [vel_x, vel_y, vel_z, str_xx, str_yy, str_zz, str_xy, str_xz, str_yz]

def reference(adjoint_state, buoyancy, lame_lambda, shear_modulus, forward_field, traces, observed, pairs, patch_basis, patch_ids, slot_counts, owner_map):
    spectrum = jnp.fft.rfft(traces, axis=2)[:, :, 1:NF + 1] / math.sqrt(NT)
    spectral_parts = jnp.stack([jnp.real(spectrum), jnp.imag(spectrum)]).astype(jnp.float32)
    spectral_parts = spectral_parts.reshape(2, STATIONS, GROUPS, BLK_DEV, NF).transpose(2, 0, 4, 3, 1).reshape(GROUPS, 2, GITEMS, STATIONS)
    first_station = pairs[:, 0]
    second_station = pairs[:, 1]
    first_spec = jnp.take(spectral_parts, first_station, axis=3)
    second_spec = jnp.take(spectral_parts, second_station, axis=3)
    cross_real = first_spec[:, 0] * second_spec[:, 0] + first_spec[:, 1] * second_spec[:, 1]
    cross_imag = first_spec[:, 0] * second_spec[:, 1] - first_spec[:, 1] * second_spec[:, 0]
    cross_spectra = jnp.stack([cross_real, cross_imag], axis=1)
    positions = jnp.arange(ITEMS).reshape(GROUPS, GITEMS).astype(jnp.float32)
    weights = 1.0 + 2.0 * positions / (ITEMS - 1)
    deviation = cross_spectra - observed
    misfit = lax.optimization_barrier(jnp.sum(weights[:, None, :, None] * deviation * deviation, axis=(0, 1, 2))) / (2.0 * ITEMS)
    station_total = jax.ops.segment_sum(misfit, first_station, STATIONS) + jax.ops.segment_sum(misfit, second_station, STATIONS)
    unit_terms = jnp.ones((PAIRS,), jnp.float32)
    station_count = jax.ops.segment_sum(unit_terms, first_station, STATIONS) + jax.ops.segment_sum(unit_terms, second_station, STATIONS)
    station_weight = station_total / jnp.maximum(station_count, 1.0)
    station_slot = jnp.arange(STATIONS) % S_DEV
    station_tile = jnp.arange(STATIONS) // S_DEV
    x_cell = (station_tile * CX + station_slot % CX).astype(jnp.int32)
    y_cell = (53 * station_slot % CY).astype(jnp.int32)
    deposit = jnp.zeros((NX, CY), jnp.float32).at[x_cell, y_cell].add(station_weight)
    fields = list(adjoint_state)
    fields[2] = fields[2].at[0].add(deposit)
    for iteration in range(ITERS):
        fields = leapfrog(fields, buoyancy, lame_lambda, shear_modulus)
    adjoint_final = jnp.stack(fields)
    kernel = fields[2] * forward_field
    slab_kernel = kernel.reshape(SLABS, CZ, NX, CY).sum(axis=1).reshape(SLABS, TILES, CX, CY)
    tile_basis = patch_basis.reshape(SLOTS, TILES, CX)
    slot_rows = jnp.einsum('jhx,dhxy->dhjy', tile_basis, slab_kernel, precision=precise_mode)
    slot_used = (jnp.arange(SLOTS)[None, :] < slot_counts[:, None]).astype(jnp.float32)
    slot_rows = slot_rows * slot_used[None, :, :, None]
    flat_rows = slot_rows.reshape(SLABS, TILES * SLOTS, CY).transpose(1, 0, 2)
    patch_sum = jax.ops.segment_sum(flat_rows, patch_ids.reshape(-1), NPATCH)
    patch_order = jnp.arange(NPATCH)
    same_owner = owner_map[:, None] == owner_map[None, :]
    earlier = patch_order[None, :] < patch_order[:, None]
    patch_rank = lax.optimization_barrier(jnp.sum((same_owner & earlier).astype(jnp.int32), axis=1))
    target = (owner_map * OWN_CAP + patch_rank).astype(jnp.int32)
    placed = jax.ops.segment_sum(patch_sum, target, TILES * OWN_CAP)
    patch_grad = placed.transpose(1, 0, 2)
    return (adjoint_final, cross_spectra, patch_grad)
```

```python
import functools
import math

import jax
import jax.numpy as jnp
import numpy as np
from jax import lax
from jax.experimental import pallas as pl
from jax.experimental.pallas import tpu as pltpu
from jax.sharding import PartitionSpec as P

ITERS = 4
CAP = 2
OWN_CAP = 8


time_step = 0.25
precise_mode = lax.Precision.HIGHEST


def with_halo(cells, sides, width):
    for axis, dim in sides:
        count = lax.axis_size(axis)
        ends = count - 1
        head = lax.slice_in_dim(cells, 0, width, axis=dim)
        tail = lax.slice_in_dim(cells, cells.shape[dim] - width, cells.shape[dim], axis=dim)
        cells = jnp.concatenate(
            [
                lax.ppermute(tail, axis, [(i, (i + 1) % count) for i in range(ends)]),
                cells,
                lax.ppermute(head, axis, [((i + 1) % count, i) for i in range(ends)]),
            ],
            axis=dim,
        )
    return cells


def forward_diff(field, along):
    extent = field.shape[along]
    ahead = jnp.concatenate(
        [
            lax.slice_in_dim(field, 1, extent, axis=along),
            jnp.zeros_like(lax.slice_in_dim(field, 0, 1, axis=along)),
        ],
        axis=along,
    )
    return ahead - field


def backward_diff(field, along):
    extent = field.shape[along]
    behind = jnp.concatenate(
        [
            jnp.zeros_like(lax.slice_in_dim(field, 0, 1, axis=along)),
            lax.slice_in_dim(field, 0, extent - 1, axis=along),
        ],
        axis=along,
    )
    return field - behind


def ahead_z(padded):
    return padded[2:, 1:-1] - padded[1:-1, 1:-1]


def behind_z(padded):
    return padded[1:-1, 1:-1] - padded[:-2, 1:-1]


def ahead_x(padded):
    return padded[1:-1, 2:] - padded[1:-1, 1:-1]


def behind_x(padded):
    return padded[1:-1, 1:-1] - padded[1:-1, :-2]


def update_stresses(
    vel_x,
    vel_y,
    vel_z,
    str_xx,
    str_yy,
    str_zz,
    str_xy,
    str_xz,
    str_yz,
    strain_xx,
    strain_zz,
    vx_ahead_z,
    vy_ahead_x,
    vy_ahead_z,
    vz_ahead_x,
    lame_lambda,
    shear_modulus,
):
    strain_yy = backward_diff(vel_y, 2)
    p_modulus = lame_lambda + 2.0 * shear_modulus
    str_xx = str_xx + time_step * (p_modulus * strain_xx + lame_lambda * (strain_yy + strain_zz))
    str_yy = str_yy + time_step * (p_modulus * strain_yy + lame_lambda * (strain_xx + strain_zz))
    str_zz = str_zz + time_step * (p_modulus * strain_zz + lame_lambda * (strain_xx + strain_yy))
    str_xy = str_xy + time_step * shear_modulus * (forward_diff(vel_x, 2) + vy_ahead_x)
    str_xz = str_xz + time_step * shear_modulus * (vx_ahead_z + vz_ahead_x)
    str_yz = str_yz + time_step * shear_modulus * (vy_ahead_z + forward_diff(vel_z, 2))
    return [vel_x, vel_y, vel_z, str_xx, str_yy, str_zz, str_xy, str_xz, str_yz]


def leapfrog(fields, buoyancy, lame_lambda, shear_modulus):
    vel_x, vel_y, vel_z, str_xx, str_yy, str_zz, str_xy, str_xz, str_yz = fields
    stress_pad = with_halo(
        jnp.stack([str_xx, str_zz, str_xy, str_xz, str_yz]), (("horiz", 2), ("depth", 1)), 1
    )
    vel_x = vel_x + time_step * buoyancy * (
        ahead_x(stress_pad[0]) + backward_diff(str_xy, 2) + behind_z(stress_pad[3])
    )
    vel_y = vel_y + time_step * buoyancy * (
        behind_x(stress_pad[2]) + forward_diff(str_yy, 2) + behind_z(stress_pad[4])
    )
    vel_z = vel_z + time_step * buoyancy * (
        behind_x(stress_pad[3]) + backward_diff(str_yz, 2) + ahead_z(stress_pad[1])
    )
    velocity_pad = with_halo(jnp.stack([vel_x, vel_y, vel_z]), (("horiz", 2), ("depth", 1)), 1)
    return update_stresses(
        vel_x,
        vel_y,
        vel_z,
        str_xx,
        str_yy,
        str_zz,
        str_xy,
        str_xz,
        str_yz,
        behind_x(velocity_pad[0]),
        behind_z(velocity_pad[2]),
        ahead_z(velocity_pad[0]),
        ahead_x(velocity_pad[1]),
        ahead_z(velocity_pad[1]),
        ahead_x(velocity_pad[2]),
        lame_lambda,
        shear_modulus,
    )


def shards(
    adjoint_state,
    buoyancy,
    lame_lambda,
    shear_modulus,
    forward_field,
    traces,
    observed,
    pairs,
    patch_basis,
    patch_ids,
    slot_counts,
    owner_map,
):
    local_stations, local_blocks, samples = traces.shape
    bin_count = samples // 2
    tile_count = lax.axis_size("horiz")
    slab_count = lax.axis_size("depth")
    tile_index = lax.axis_index("horiz")
    depth_index = lax.axis_index("depth")
    stations = local_stations * tile_count
    group_items = local_blocks * bin_count
    items_dev = group_items // tile_count
    n_pairs = pairs.shape[0]
    x_cells = forward_field.shape[1]
    y_cells = forward_field.shape[2]
    sample_index = lax.iota(jnp.int32, samples)
    frequency = lax.iota(jnp.int32, bin_count) + 1
    phases = sample_index[:, None] * frequency[None, :] % samples
    angles = phases.astype(jnp.float32) * (2.0 * math.pi / samples)
    fourier_table = jnp.concatenate([jnp.cos(angles), -jnp.sin(angles)], axis=1) / math.sqrt(
        samples
    )
    spectra = jnp.einsum("sbt,tm->mbs", traces, fourier_table, precision=precise_mode)
    spectra = spectra.reshape(2, tile_count, items_dev, local_stations)
    first_station = pairs[:, 0]
    second_station = pairs[:, 1]
    received_block = lax.all_to_all(spectra, "horiz", split_axis=1, concat_axis=3, tiled=True)[:, 0]
    first_spec = jnp.take(received_block, first_station, axis=2)
    second_spec = jnp.take(received_block, second_station, axis=2)
    cross_real = first_spec[0] * second_spec[0] + first_spec[1] * second_spec[1]
    cross_imag = first_spec[0] * second_spec[1] - first_spec[1] * second_spec[0]
    cross = jnp.stack([cross_real, cross_imag])
    items_all = group_items * slab_count
    positions = (
        depth_index * group_items + tile_index * items_dev + lax.iota(jnp.int32, items_dev)
    ).astype(jnp.float32)
    weights = 1.0 + 2.0 * positions / (items_all - 1)
    deviation = cross - observed[0]
    pair_terms = jnp.sum(weights[None, :, None] * deviation * deviation, axis=(0, 1)) / (
        2.0 * items_all
    )
    all_terms = lax.psum(pair_terms, ("horiz", "depth"))
    total_all = jax.ops.segment_sum(all_terms, first_station, stations) + jax.ops.segment_sum(
        all_terms, second_station, stations
    )
    station_total = lax.dynamic_slice_in_dim(total_all, tile_index * local_stations, local_stations)
    unit_terms = jnp.ones((n_pairs,), jnp.float32)
    count_all = jax.ops.segment_sum(unit_terms, first_station, stations) + jax.ops.segment_sum(
        unit_terms, second_station, stations
    )
    station_count = lax.dynamic_slice_in_dim(count_all, tile_index * local_stations, local_stations)
    station_weight = station_total / jnp.maximum(station_count, 1.0)
    station_slot = lax.iota(jnp.int32, local_stations)
    onehot_x = ((station_slot % x_cells)[:, None] == lax.iota(jnp.int32, x_cells)[None, :]).astype(
        jnp.float32
    )
    onehot_y = (
        (53 * station_slot % y_cells)[:, None] == lax.iota(jnp.int32, y_cells)[None, :]
    ).astype(jnp.float32)
    deposit = jnp.dot((station_weight[:, None] * onehot_x).T, onehot_y, precision=precise_mode)
    surface = (depth_index == 0).astype(jnp.float32)
    fields = list(adjoint_state)
    fields[2] = fields[2].at[0].add(surface * deposit)
    for iteration in range(ITERS):
        fields = leapfrog(fields, buoyancy, lame_lambda, shear_modulus)
    adjoint_final = jnp.stack(fields)
    kernel = jnp.sum(fields[2] * forward_field, axis=0)
    slot_rows = jnp.dot(patch_basis, kernel, precision=precise_mode)
    n_slots = patch_ids.shape[1]
    n_patch = owner_map.shape[0]
    slot_used = lax.iota(jnp.int32, n_slots) < slot_counts[0]
    slot_ids = patch_ids[0]
    patch_order = lax.iota(jnp.int32, n_patch)
    same_owner = owner_map[:, None] == owner_map[None, :]
    earlier = patch_order[None, :] < patch_order[:, None]
    patch_rank = jnp.sum((same_owner & earlier).astype(jnp.int32), axis=1)
    rank_slots = lax.iota(jnp.int32, OWN_CAP)
    target = owner_map[slot_ids]
    dest_hot = (
        (target[:, None] == lax.iota(jnp.int32, tile_count)[None, :]) & slot_used[:, None]
    ).astype(jnp.int32)
    running = jnp.cumsum(dest_hot, axis=0) - 1
    position = jnp.sum(dest_hot * running, axis=1)
    buffer_index = target * CAP + position
    selector = (
        lax.iota(jnp.int32, tile_count * CAP)[:, None] == buffer_index[None, :]
    ) & slot_used[None, :]
    send_rows = jnp.dot(selector.astype(jnp.float32), slot_rows, precision=precise_mode).reshape(
        tile_count, CAP, y_cells
    )
    send_ids = jnp.sum(jnp.where(selector, slot_ids[None, :], 0), axis=1).reshape(tile_count, CAP)
    got_rows, got_ids = (
        lax.all_to_all(send_rows, "horiz", split_axis=0, concat_axis=0, tiled=True),
        lax.all_to_all(send_ids, "horiz", split_axis=0, concat_axis=0, tiled=True),
    )
    got_rows = got_rows.reshape(tile_count * CAP, y_cells)
    got_ids = got_ids.reshape(tile_count * CAP)
    placing = (
        (patch_rank[got_ids][None, :] == rank_slots[:, None])
        & (owner_map[got_ids] == tile_index)[None, :]
    ).astype(jnp.float32)
    patch_grad = jnp.dot(placing, got_rows, precision=precise_mode)
    return (adjoint_final, cross[None], patch_grad[None])


LEV, XC, YC, STN, BLK, FREQ = 8, 16, 128, 32, 8, 8
VX, VY, VZ, SXX, SYY, SZZ, SXY, SXZ, SYZ, BUO, LAM, MU = range(12)
EXT_X = XC + 8
FIRST = 5
CHUNKS = 6
EARLY = 3
WIDE = 2
ALL_VMEM = 67043328
SPARE = 2**11
MESH = pl.DeviceIdType.MESH


def split3(value):
    high = value.astype(jnp.bfloat16)
    rest = value - high.astype(jnp.float32)
    mid = rest.astype(jnp.bfloat16)
    low = (rest - mid.astype(jnp.float32)).astype(jnp.bfloat16)
    return high, mid, low


def dot32(a, b, dims):
    return lax.dot_general(
        a, b, (dims, ((), ())), precision=precise_mode, preferred_element_type=jnp.float32
    )


def roll_x(f, up):
    return pltpu.roll(f, EXT_X - 1 if up else 1, 0)


def velocity_levels(ext, mats, first, count):
    lane = lax.broadcasted_iota(jnp.int32, (EXT_X, YC), 1)

    def ahead_y(f):
        return jnp.where(lane == YC - 1, 0.0, pltpu.roll(f, YC - 1, 1)) - f

    def behind_y(f):
        return f - jnp.where(lane == 0, 0.0, pltpu.roll(f, 1, 1))

    results = []
    for i in range(count):
        z = first + i
        sxy = ext[SXY, z]
        sxz = ext[SXZ, z]
        syz = ext[SYZ, z]
        sxx = ext[SXX, z]
        scale = time_step * mats[BUO, z]
        vx = ext[VX, z] + scale * (
            (roll_x(sxx, True) - sxx) + behind_y(sxy) + (sxz - ext[SXZ, z - 1])
        )
        vy = ext[VY, z] + scale * (
            (sxy - roll_x(sxy, False)) + ahead_y(ext[SYY, z]) + (syz - ext[SYZ, z - 1])
        )
        vz = ext[VZ, z] + scale * (
            (sxz - roll_x(sxz, False)) + behind_y(syz) + (ext[SZZ, z + 1] - ext[SZZ, z])
        )
        results.append((vx, vy, vz))
    for i in range(count):
        for k, value in zip((VX, VY, VZ), results[i]):
            ext[k, first + i] = value


def stress_levels(ext, mats, first, count):
    lane = lax.broadcasted_iota(jnp.int32, (EXT_X, YC), 1)

    def ahead_y(f):
        return jnp.where(lane == YC - 1, 0.0, pltpu.roll(f, YC - 1, 1)) - f

    def behind_y(f):
        return f - jnp.where(lane == 0, 0.0, pltpu.roll(f, 1, 1))

    results = []
    for i in range(count):
        z = first + i
        vx = ext[VX, z]
        vy = ext[VY, z]
        vz = ext[VZ, z]
        lam = time_step * mats[LAM, z]
        mu = time_step * mats[MU, z]
        exx = vx - roll_x(vx, False)
        eyy = behind_y(vy)
        ezz = vz - ext[VZ, z - 1]
        p_mod = lam + 2.0 * mu
        sxx = ext[SXX, z] + (p_mod * exx + lam * (eyy + ezz))
        syy = ext[SYY, z] + (p_mod * eyy + lam * (exx + ezz))
        szz = ext[SZZ, z] + (p_mod * ezz + lam * (exx + eyy))
        sxy = ext[SXY, z] + mu * (ahead_y(vx) + (roll_x(vy, True) - vy))
        sxz = ext[SXZ, z] + mu * ((ext[VX, z + 1] - vx) + (roll_x(vz, True) - vz))
        syz = ext[SYZ, z] + mu * ((ext[VY, z + 1] - vy) + ahead_y(vz))
        results.append((sxx, syy, szz, sxy, sxz, syz))
    for i in range(count):
        for k, value in zip((SXX, SYY, SZZ, SXY, SXZ, SYZ), results[i]):
            ext[k, first + i] = value


def fused_kernel(
    tiles,
    slabs,
    state_ref,
    buo_ref,
    lam_ref,
    mu_ref,
    forward_hbm,
    traces_hbm,
    observed_hbm,
    pairs_hbm,
    basis_hbm,
    ids_hbm,
    counts_hbm,
    owner_hbm,
    table_hbm,
    ext,
    cross_ref,
    grad_ref,
    forward_ref,
    traces_ref,
    observed_ref,
    pairs_ref,
    basis_ref,
    ids_ref,
    counts_ref,
    owner_ref,
    table_ref,
    pack_r,
    pack_l,
    halo_r,
    halo_l,
    spec_out,
    spec_in,
    left_rows,
    right_rows,
    part,
    parts,
    added,
    rows_out,
    rows_in,
    local_sem,
    spec_send,
    spec_recv,
    slab_send,
    slab_recv,
    side_send,
    side_recv,
    corner_send,
    corner_recv,
    part_send,
    part_recv,
    row_send,
    row_recv,
    far_sem,
):
    me = lax.axis_index("horiz")
    depth = lax.axis_index("depth")
    n_pairs = pairs_ref.shape[1]
    own = pl.ds(FIRST, LEV)
    arrays = ((0, 9, state_ref), (9, 1, buo_ref), (10, 1, lam_ref), (11, 1, mu_ref))
    pair_rows = tiles // WIDE
    row_z, row_y = me // WIDE, lax.rem(me, WIDE)

    barrier = pltpu.get_barrier_semaphore()
    for d in range(1, slabs):
        other = {"depth": lax.rem(depth + d, slabs)}
        pl.semaphore_signal(barrier, inc=1, device_id=other, device_id_type=MESH)
    for k in range(1, WIDE):
        other = {"horiz": row_z * WIDE + lax.rem(row_y + k, WIDE)}
        pl.semaphore_signal(barrier, inc=1, device_id=other, device_id_type=MESH)

    def near_rows(run):
        for step in (-1, 1):

            @pl.when((row_z + step >= 0) & (row_z + step < pair_rows))
            def _():
                run(step)

    def greet(step):
        for k in range(WIDE):
            other = {"horiz": (row_z + step) * WIDE + k}
            pl.semaphore_signal(barrier, inc=1, device_id=other, device_id_type=MESH)

    near_rows(greet)

    smalls = (
        (traces_hbm, traces_ref),
        (table_hbm, table_ref),
        (pairs_hbm, pairs_ref),
        (basis_hbm, basis_ref),
        (ids_hbm, ids_ref),
        (counts_hbm, counts_ref),
        (owner_hbm, owner_ref),
        (observed_hbm, observed_ref),
        (forward_hbm, forward_ref),
    )
    small_in = [
        pltpu.make_async_copy(src, dst, local_sem.at[4 + n]) for n, (src, dst) in enumerate(smalls)
    ]
    locals_in = [
        pltpu.make_async_copy(
            src, ext.at[pl.ds(start, count), own, pl.ds(0, XC)], local_sem.at[n]
        )
        for n, (start, count, src) in enumerate(arrays)
    ]
    for copy in small_in[:2] + locals_in + small_in[2:]:
        copy.start()

    row = lax.broadcasted_iota(jnp.int32, (8, YC), 0)
    lower = row < 4
    for copy in small_in[:2]:
        copy.wait()
    by_block = jnp.concatenate(
        [traces_ref[pl.ds(b, STN, stride=BLK), :] for b in range(BLK)], axis=0
    )
    spectra = dot32(table_ref[...], by_block, ((1,), (1,)))
    half = tiles * FREQ
    for t in range(tiles):
        for c in range(2):
            spec_out[t, pl.ds(c * FREQ, FREQ), :] = spectra[
                c * half + t * FREQ : c * half + (t + 1) * FREQ
            ]
    for copy in locals_in:
        copy.wait()

    def pack_one(a, carry):
        for j in range(LEV // 2):
            even, odd = FIRST + 2 * j, FIRST + 2 * j + 1
            pack_r[a, j] = jnp.where(
                lower, ext[a, even, pl.ds(0, 8)], pltpu.roll(ext[a, odd, pl.ds(0, 8)], 4, 0)
            )
            pack_l[a, j] = jnp.where(
                lower, pltpu.roll(ext[a, odd, pl.ds(8, 8)], 4, 0), ext[a, even, pl.ds(8, 8)]
            )
        return carry

    lax.fori_loop(0, 12, pack_one, 0)

    mid_pairs = pl.ds(2, LEV // 2)

    def side_copy(n, c):
        source, target, step = ((pack_r, halo_r, -1), (pack_l, halo_l, 1))[n]
        some = pl.ds(c * 12 // CHUNKS, 12 // CHUNKS)
        return pltpu.make_async_remote_copy(
            src_ref=source.at[some],
            dst_ref=target.at[some, mid_pairs],
            send_sem=side_send.at[n, c],
            recv_sem=side_recv.at[n, c],
            device_id={"horiz": me + step},
            device_id_type=MESH,
        )

    def slab_copy(n, m):
        start, count, src = arrays[m]
        levels = pl.ds(0, 4) if n == 0 else pl.ds(LEV - 4, 4)
        source = src.at[:, levels]
        target = ext.at[
            pl.ds(start, count), pl.ds(FIRST + LEV if n == 0 else FIRST - 4, 4), pl.ds(0, XC)
        ]
        return pltpu.make_async_remote_copy(
            src_ref=source,
            dst_ref=target,
            send_sem=slab_send.at[n, m],
            recv_sem=slab_recv.at[n, m],
            device_id={"depth": depth + (-1 if n == 0 else 1)},
            device_id_type=MESH,
        )

    def corner_copy(n, m, c):
        buffer = (halo_r, halo_l)[m]
        some = pl.ds(c * 12 // CHUNKS, 12 // CHUNKS)
        return pltpu.make_async_remote_copy(
            src_ref=buffer.at[some, pl.ds(2 if n == 0 else 4, 2)],
            dst_ref=buffer.at[some, pl.ds(6 if n == 0 else 0, 2)],
            send_sem=corner_send.at[n, m, c],
            recv_sem=corner_recv.at[n, m, c],
            device_id={"depth": depth + (-1 if n == 0 else 1)},
            device_id_type=MESH,
        )

    has_left, has_right = me > 0, me < tiles - 1
    has_up, has_down = depth > 0, depth < slabs - 1

    def side_start(c):
        @pl.when(has_left)
        def _():
            side_copy(0, c).start()

        @pl.when(has_right)
        def _():
            side_copy(1, c).start()

    def spec_copy(peer, source):
        return pltpu.make_async_remote_copy(
            src_ref=spec_out.at[peer],
            dst_ref=spec_in.at[source],
            send_sem=spec_send.at[peer],
            recv_sem=spec_recv.at[source],
            device_id={"horiz": peer},
            device_id_type=MESH,
        )

    def far_signal(step, stage):
        pl.semaphore_signal(
            far_sem.at[(step + 1) // 2, stage],
            inc=1,
            device_id={"horiz": me + step * WIDE},
            device_id_type=MESH,
        )

    def spec_row(distance):
        for step in (-1, 1):
            there = row_z + step * distance

            @pl.when((there >= 0) & (there < pair_rows))
            def _():
                for k in range(WIDE):
                    spec_copy(there * WIDE + k, me).start()

    pl.semaphore_wait(
        barrier,
        slabs
        - 1
        + WIDE
        - 1
        + jnp.where(row_z > 0, WIDE, 0)
        + jnp.where(row_z < pair_rows - 1, WIDE, 0),
    )
    for step in (-1, 1):

        @pl.when(
            (row_z - step >= 0)
            & (row_z - step < pair_rows)
            & (row_z + step >= 0)
            & (row_z + step < pair_rows)
        )
        def _():
            far_signal(step, 0)

    for c in range(EARLY):
        side_start(c)

    @pl.when(has_up)
    def _():
        for m in range(4):
            slab_copy(0, m).start()

    @pl.when(has_down)
    def _():
        for m in range(4):
            slab_copy(1, m).start()

    for k in range(1, WIDE):
        spec_copy(row_z * WIDE + lax.rem(row_y + k, WIDE), me).start()
    spec_row(1)
    for distance in range(2, pair_rows):
        for step in (-1, 1):
            source = row_z - step * distance
            after = row_z + step

            @pl.when((source >= 0) & (source < pair_rows))
            def _():
                pl.semaphore_wait(far_sem.at[(step + 1) // 2, distance - 2], 1)
                if distance < pair_rows - 1:

                    @pl.when((after >= 0) & (after < pair_rows))
                    def _():
                        far_signal(step, distance - 1)

        spec_row(distance)
    for c in range(EARLY, CHUNKS):
        side_start(c)
    spec_in[me] = spec_out[me]

    def clear_levels(first):
        def clear(a, carry):
            for i in range(4):
                ext[a, first + i] = jnp.zeros((EXT_X, YC), jnp.float32)
            return carry

        lax.fori_loop(0, 12, clear, 0)

    def clear_pairs(buffer, first, count):
        def clear(a, carry):
            for i in range(count):
                buffer[a, first + i] = jnp.zeros((8, YC), jnp.float32)
            return carry

        lax.fori_loop(0, 12, clear, 0)

    @pl.when(jnp.logical_not(has_up))
    def _():
        clear_levels(FIRST - 4)
        clear_pairs(halo_r, 0, 2)
        clear_pairs(halo_l, 0, 2)

    @pl.when(jnp.logical_not(has_down))
    def _():
        clear_levels(FIRST + LEV)
        clear_pairs(halo_r, 6, 2)
        clear_pairs(halo_l, 6, 2)

    @pl.when(jnp.logical_not(has_right))
    def _():
        clear_pairs(halo_r, 2, 4)

    @pl.when(jnp.logical_not(has_left))
    def _():
        clear_pairs(halo_l, 2, 4)

    def clear_ends(a, carry):
        ext[a, 0] = jnp.zeros((EXT_X, YC), jnp.float32)
        ext[a, 17] = jnp.zeros((EXT_X, YC), jnp.float32)
        return carry

    lax.fori_loop(0, 12, clear_ends, 0)

    def clear_added(a, carry):
        for i in range(ITERS + 3):
            added[a, FIRST - 1 + i] = jnp.zeros((EXT_X, YC), jnp.float32)
        return carry

    @pl.when(depth == 0)
    def _():
        lax.fori_loop(0, 9, clear_added, 0)

    for copy in small_in[2:7]:
        copy.wait()
    first_pair = pairs_ref[pl.ds(0, 1), :]
    second_pair = pairs_ref[pl.ds(1, 1), :]
    stations = tiles * STN
    station = lax.broadcasted_iota(jnp.int32, (stations, n_pairs), 0)
    hot_first = (station == first_pair).astype(jnp.float32).astype(jnp.bfloat16)
    hot_second = (station == second_pair).astype(jnp.float32).astype(jnp.bfloat16)
    n_patch = owner_ref.shape[1]
    n_slots = ids_ref.shape[1]
    owner_row = owner_ref[...]
    up_iota = lax.broadcasted_iota(jnp.int32, (n_patch, n_patch), 0)
    across = lax.broadcasted_iota(jnp.int32, (n_patch, n_patch), 1)
    owner_wide = jnp.broadcast_to(owner_row, (n_patch, n_patch))
    owner_col = jnp.sum(jnp.where(up_iota == across, owner_wide, 0), axis=1, keepdims=True)
    rank_row = jnp.sum(
        jnp.where((owner_col == owner_wide) & (up_iota < across), 1, 0), axis=0, keepdims=True
    )
    target_row = owner_row * OWN_CAP + rank_row
    out_rows = tiles * OWN_CAP
    place = (
        lax.broadcasted_iota(jnp.int32, (out_rows, n_patch), 0) == target_row
    ).astype(jnp.float32)
    slot = lax.broadcasted_iota(jnp.int32, (n_patch, n_slots), 1)
    patch = lax.broadcasted_iota(jnp.int32, (n_patch, n_slots), 0)
    named = ((patch == ids_ref[...]) & (slot < counts_ref[...])).astype(jnp.float32)
    slot_place = dot32(place, named, ((1,), (0,)))
    row_basis = dot32(slot_place, basis_ref[...], ((1,), (0,)))

    for k in range(1, tiles):
        source = lax.rem(me + k, tiles)
        spec_copy(me, source).wait_recv()
    small_in[7].wait()
    for b in range(BLK):
        wide = jnp.concatenate(
            [spec_in[t][:, b * STN : (b + 1) * STN] for t in range(tiles)], axis=1
        )
        left_rows[pl.ds(b * 2 * FREQ, 2 * FREQ), :] = wide[:, :128]
        right_rows[pl.ds(b * 2 * FREQ, 2 * FREQ), :] = wide[:, 128:]
    ordered = jnp.concatenate(
        [
            jnp.concatenate(
                [r[pl.ds(cf, BLK, stride=2 * FREQ), :] for cf in range(2 * FREQ)], axis=0
            )
            for r in (left_rows, right_rows)
        ],
        axis=1,
    )
    pieces = split3(ordered)

    def gather(hot):
        return sum(
            lax.dot_general(
                piece, hot, (((1,), (0,)), ((), ())), preferred_element_type=jnp.float32
            )
            for piece in pieces[::-1]
        )

    first_spec = gather(hot_first)
    second_spec = gather(hot_second)
    items = FREQ * BLK
    f_re, f_im = first_spec[:items], first_spec[items:]
    s_re, s_im = second_spec[:items], second_spec[items:]
    cross_re = f_re * s_re + f_im * s_im
    cross_im = f_re * s_im - f_im * s_re
    items_all = items * tiles * slabs
    item = lax.broadcasted_iota(jnp.int32, (items, 1), 0) + (depth * tiles + me) * items
    weight = 1.0 + 2.0 * item.astype(jnp.float32) / (items_all - 1)
    dev_re = cross_re - observed_ref[0, 0]
    dev_im = cross_im - observed_ref[0, 1]
    terms = weight * (dev_re * dev_re + dev_im * dev_im)
    part[...] = jnp.sum(terms, axis=0, keepdims=True)

    def part_copy(d, k, receiving=False):
        slot = d * tiles + (lax.rem(me + tiles - k, tiles) if receiving else me)
        return pltpu.make_async_remote_copy(
            src_ref=part,
            dst_ref=parts.at[slot],
            send_sem=part_send.at[k],
            recv_sem=part_recv.at[d, k],
            device_id={"horiz": lax.rem(me + k, tiles), "depth": 0},
            device_id_type=MESH,
        )

    for k in range(1, tiles):
        part_copy(depth, k).start()

    @pl.when(depth > 0)
    def _():
        part_copy(depth, 0).start()

    cross_ref[0, 0] = cross_re
    cross_ref[0, 1] = cross_im

    for c in range(CHUNKS):

        @pl.when(has_left)
        def _():
            side_copy(1, c).wait_recv()

        @pl.when(has_right)
        def _():
            side_copy(0, c).wait_recv()

        @pl.when(has_up)
        def _():
            for m in range(2):
                corner_copy(0, m, c).start()

        @pl.when(has_down)
        def _():
            for m in range(2):
                corner_copy(1, m, c).start()

    def unpack(first, count):
        def unpack_one(a, carry):
            for j in range(first, first + count):
                r, l = halo_r[a, j], halo_l[a, j]
                ext[a, 1 + 2 * j, pl.ds(XC, 8)] = jnp.where(lower, r, l)
                ext[a, 2 + 2 * j, pl.ds(XC, 8)] = pltpu.roll(jnp.where(lower, l, r), 4, 0)
            return carry

        lax.fori_loop(0, 12, unpack_one, 0)

    unpack(2, 4)

    @pl.when(has_up)
    def _():
        for m in range(4):
            slab_copy(1, m).wait_recv()
        for m in range(2):
            for c in range(CHUNKS):
                corner_copy(1, m, c).wait_recv()

    @pl.when(has_down)
    def _():
        for m in range(4):
            slab_copy(0, m).wait_recv()
        for m in range(2):
            for c in range(CHUNKS):
                corner_copy(0, m, c).wait_recv()

    unpack(0, 2)
    unpack(6, 2)

    for n in range(ITERS):

        def v_body(i, carry):
            velocity_levels(ext, ext, 1 + n + 2 * i, 2)
            return carry

        def s_body(i, carry):
            stress_levels(ext, ext, 2 + n + 2 * i, 2)
            return carry

        lax.fori_loop(0, 8 - n, v_body, 0)
        lax.fori_loop(0, 7 - n, s_body, 0)

    @pl.when(depth == 0)
    def _():
        for d in range(slabs):
            for k in range(tiles):
                if d or k:
                    part_copy(d, k, True).wait_recv()
        parts[me] = part[...]
        total = parts[0]
        for t in range(1, tiles * slabs):
            total = total + parts[t]
        terms = total / (2.0 * items_all)
        ext_row = lax.broadcasted_iota(jnp.int32, (EXT_X, 1), 0)
        x = me * XC + jnp.where(ext_row < XC + 4, ext_row, ext_row - EXT_X)
        x_pos = x + XC
        tile = x_pos // XC - 1
        in_tile = x_pos - (tile + 1) * XC
        lane = lax.broadcasted_iota(jnp.int32, (EXT_X, YC), 1)
        deposit = jnp.zeros((EXT_X, YC), jnp.float32)
        for turn in range(STN // XC):
            within = in_tile + turn * XC
            index = tile * STN + within
            hits = (index == first_pair).astype(jnp.float32) + (index == second_pair).astype(
                jnp.float32
            )
            sums = jnp.sum(hits * terms, axis=1, keepdims=True)
            number = jnp.sum(hits, axis=1, keepdims=True)
            value = sums / jnp.maximum(number, 1.0)
            deposit = deposit + jnp.where(lane == lax.rem(53 * within, YC), value, 0.0)
        added[VZ, FIRST] = deposit
        for n in range(ITERS):
            if n:
                for z in range(0, n + 1, 2):
                    velocity_levels(added, ext, FIRST + z, min(2, n + 1 - z))
            for z in range(0, n + 2, 2):
                stress_levels(added, ext, FIRST + z, min(2, n + 2 - z))

        def add_one(a, carry):
            for i in range(ITERS + 1):
                ext[a, FIRST + i, pl.ds(0, XC)] += added[a, FIRST + i, pl.ds(0, XC)]
            return carry

        lax.fori_loop(0, 9, add_one, 0)

    small_in[8].wait()
    slab = sum(ext[VZ, FIRST + i, pl.ds(0, XC)] * forward_ref[i] for i in range(LEV))
    rows = dot32(row_basis, slab, ((1,), (0,)))
    for t in range(tiles):
        rows_out[t] = rows[t * OWN_CAP : (t + 1) * OWN_CAP]
    row_copies = []
    for k in range(1, tiles):
        peer = lax.rem(me + k, tiles)
        row_copies.append(
            pltpu.make_async_remote_copy(
                src_ref=rows_out.at[peer],
                dst_ref=rows_in.at[me],
                send_sem=row_send.at[k],
                recv_sem=row_recv.at[k],
                device_id={"horiz": peer},
                device_id_type=MESH,
            )
        )
    for copy in row_copies:
        copy.start()
    rows_in[me] = rows_out[me]

    for k in range(1, tiles):
        spec_copy(lax.rem(me + k, tiles), me).wait_send()

    @pl.when(has_left)
    def _():
        for c in range(CHUNKS):
            side_copy(0, c).wait_send()

    @pl.when(has_right)
    def _():
        for c in range(CHUNKS):
            side_copy(1, c).wait_send()

    @pl.when(has_up)
    def _():
        for m in range(4):
            slab_copy(0, m).wait_send()
        for m in range(2):
            for c in range(CHUNKS):
                corner_copy(0, m, c).wait_send()

    @pl.when(has_down)
    def _():
        for m in range(4):
            slab_copy(1, m).wait_send()
        for m in range(2):
            for c in range(CHUNKS):
                corner_copy(1, m, c).wait_send()

    for k in range(1, tiles):
        part_copy(depth, k).wait_send()

    @pl.when(depth > 0)
    def _():
        part_copy(depth, 0).wait_send()

    for copy in row_copies:
        copy.wait_recv()
    grad_ref[0] = sum(rows_in[t] for t in range(tiles))
    for copy in row_copies:
        copy.wait_send()


def hand_out_kernel(ext, cross, grad, final_ref, cross_ref, grad_ref, out_sem):
    own = pl.ds(FIRST, LEV)
    writes = [
        pltpu.make_async_copy(src, dst, out_sem.at[n])
        for n, (src, dst) in enumerate(
            (
                (ext.at[pl.ds(0, 9), own, pl.ds(0, XC)], final_ref),
                (cross, cross_ref),
                (grad, grad_ref),
            )
        )
    ]
    for write in writes:
        write.start()
    for write in writes:
        write.wait()


def hand_out(state, ext, cross, grad):
    anywhere = pl.BlockSpec(memory_space=pl.ANY)
    f32 = jnp.float32
    return pl.pallas_call(
        hand_out_kernel,
        out_shape=(
            jax.ShapeDtypeStruct(state.shape, f32),
            jax.ShapeDtypeStruct(cross.shape, f32),
            jax.ShapeDtypeStruct(grad.shape, f32),
        ),
        in_specs=[pl.BlockSpec(memory_space=pltpu.VMEM)] * 3,
        out_specs=(anywhere,) * 3,
        scratch_shapes=[pltpu.SemaphoreType.DMA((3,))],
        compiler_params=pltpu.CompilerParams(vmem_limit_bytes=2**20),
    )(ext, cross, grad)


def fused_shards(
    adjoint_state,
    buoyancy,
    lame_lambda,
    shear_modulus,
    forward_field,
    traces,
    observed,
    pairs,
    patch_basis,
    patch_ids,
    slot_counts,
    owner_map,
):
    tiles, slabs = lax.axis_size("horiz"), lax.axis_size("depth")
    samples = traces.shape[2]
    n_pairs = pairs.shape[0]
    bins = samples // 2
    phases = np.outer(np.arange(1, bins + 1), np.arange(samples)) % samples
    angles = phases * (2.0 * math.pi / samples)
    table = np.concatenate([np.cos(angles), -np.sin(angles)], axis=0) / math.sqrt(samples)
    vmem = pl.BlockSpec(memory_space=pltpu.VMEM)
    anywhere = pl.BlockSpec(memory_space=pl.ANY)
    f32 = jnp.float32
    dma = pltpu.SemaphoreType.DMA
    kept = 4 * (12 * (LEV + 10) * EXT_X * YC + math.prod(observed.shape) + OWN_CAP * YC) + SPARE
    return pl.pallas_call(
        functools.partial(fused_kernel, tiles, slabs),
        out_shape=(
            pltpu.VMEM((12, LEV + 10, EXT_X, YC), f32),
            pltpu.VMEM(observed.shape, f32),
            pltpu.VMEM((1, OWN_CAP, YC), f32),
        ),
        in_specs=[anywhere] * 13,
        out_specs=(vmem, vmem, vmem),
        scratch_shapes=[
            pltpu.VMEM(forward_field.shape, f32),
            pltpu.VMEM((STN * BLK, samples), f32),
            pltpu.VMEM(observed.shape, f32),
            pltpu.VMEM((2, n_pairs), jnp.int32),
            pltpu.VMEM(patch_basis.shape, f32),
            pltpu.VMEM(patch_ids.shape, jnp.int32),
            pltpu.VMEM((1, 1), jnp.int32),
            pltpu.VMEM((1, owner_map.shape[0]), jnp.int32),
            pltpu.VMEM(table.shape, f32),
            pltpu.VMEM((12, 4, 8, YC), f32),
            pltpu.VMEM((12, 4, 8, YC), f32),
            pltpu.VMEM((12, 8, 8, YC), f32),
            pltpu.VMEM((12, 8, 8, YC), f32),
            pltpu.VMEM((tiles, 2 * FREQ, BLK * STN), f32),
            pltpu.VMEM((tiles, 2 * FREQ, BLK * STN), f32),
            pltpu.VMEM((2 * FREQ * BLK, 128), f32),
            pltpu.VMEM((2 * FREQ * BLK, 128), f32),
            pltpu.VMEM((1, n_pairs), f32),
            pltpu.VMEM((tiles * slabs, 1, n_pairs), f32),
            pltpu.VMEM((9, FIRST + ITERS + 2, EXT_X, YC), f32),
            pltpu.VMEM((tiles, OWN_CAP, YC), f32),
            pltpu.VMEM((tiles, OWN_CAP, YC), f32),
            dma((13,)),
            dma((tiles,)),
            dma((tiles,)),
            dma((2, 4)),
            dma((2, 4)),
            dma((2, CHUNKS)),
            dma((2, CHUNKS)),
            dma((2, 2, CHUNKS)),
            dma((2, 2, CHUNKS)),
            dma((tiles,)),
            dma((slabs, tiles)),
            dma((tiles,)),
            dma((tiles,)),
            pltpu.SemaphoreType.REGULAR((2, max(tiles // WIDE - 2, 1))),
        ],
        compiler_params=pltpu.CompilerParams(
            collective_id=0, has_side_effects=True, vmem_limit_bytes=ALL_VMEM - kept
        ),
    )(
        adjoint_state,
        buoyancy[None],
        lame_lambda[None],
        shear_modulus[None],
        forward_field,
        traces.reshape(-1, samples),
        observed,
        pairs.T,
        patch_basis,
        patch_ids,
        slot_counts.reshape(1, 1),
        owner_map.reshape(1, -1),
        jnp.asarray(table, f32),
    )


def fits_fused(tiles, slabs, state, traces, pairs):
    return (
        state[1:] == (LEV, XC, YC)
        and traces == (STN, BLK, 128)
        and tiles * FREQ == 64
        and slabs > 1
        and pairs[0] % 128 == 0
    )


def local_program(*args):
    tiles, slabs = lax.axis_size("horiz"), lax.axis_size("depth")
    if fits_fused(tiles, slabs, args[0].shape, args[5].shape, args[7].shape):
        return hand_out(args[0], *fused_shards(*args))
    return shards(*args)


def solution(mesh):
    return jax.shard_map(
        local_program,
        mesh=mesh,
        in_specs=(
            P(None, "depth", "horiz", None),
            P("depth", "horiz", None),
            P("depth", "horiz", None),
            P("depth", "horiz", None),
            P("depth", "horiz", None),
            P("horiz", "depth", None),
            P("depth", None, "horiz", None),
            P(),
            P(None, "horiz"),
            P("horiz", None),
            P("horiz"),
            P(),
        ),
        out_specs=(
            P(None, "depth", "horiz", None),
            P("depth", None, "horiz", None),
            P("depth", "horiz", None),
        ),
        check_vma=False,
    )
```

```python
import functools
import math

import jax
import jax.numpy as jnp
import numpy as np
from jax import lax
from jax.experimental import pallas as pl
from jax.experimental.pallas import tpu as pltpu
from jax.sharding import PartitionSpec as P

ITERS = 4
CAP = 2
OWN_CAP = 8


time_step = 0.25
precise_mode = lax.Precision.HIGHEST


def with_halo(cells, sides, width):
    for axis, dim in sides:
        count = lax.axis_size(axis)
        ends = count - 1
        head = lax.slice_in_dim(cells, 0, width, axis=dim)
        tail = lax.slice_in_dim(cells, cells.shape[dim] - width, cells.shape[dim], axis=dim)
        cells = jnp.concatenate(
            [
                lax.ppermute(tail, axis, [(i, (i + 1) % count) for i in range(ends)]),
                cells,
                lax.ppermute(head, axis, [((i + 1) % count, i) for i in range(ends)]),
            ],
            axis=dim,
        )
    return cells


def forward_diff(field, along):
    extent = field.shape[along]
    ahead = jnp.concatenate(
        [
            lax.slice_in_dim(field, 1, extent, axis=along),
            jnp.zeros_like(lax.slice_in_dim(field, 0, 1, axis=along)),
        ],
        axis=along,
    )
    return ahead - field


def backward_diff(field, along):
    extent = field.shape[along]
    behind = jnp.concatenate(
        [
            jnp.zeros_like(lax.slice_in_dim(field, 0, 1, axis=along)),
            lax.slice_in_dim(field, 0, extent - 1, axis=along),
        ],
        axis=along,
    )
    return field - behind


def ahead_z(padded):
    return padded[2:, 1:-1] - padded[1:-1, 1:-1]


def behind_z(padded):
    return padded[1:-1, 1:-1] - padded[:-2, 1:-1]


def ahead_x(padded):
    return padded[1:-1, 2:] - padded[1:-1, 1:-1]


def behind_x(padded):
    return padded[1:-1, 1:-1] - padded[1:-1, :-2]


def update_stresses(
    vel_x,
    vel_y,
    vel_z,
    str_xx,
    str_yy,
    str_zz,
    str_xy,
    str_xz,
    str_yz,
    strain_xx,
    strain_zz,
    vx_ahead_z,
    vy_ahead_x,
    vy_ahead_z,
    vz_ahead_x,
    lame_lambda,
    shear_modulus,
):
    strain_yy = backward_diff(vel_y, 2)
    p_modulus = lame_lambda + 2.0 * shear_modulus
    str_xx = str_xx + time_step * (p_modulus * strain_xx + lame_lambda * (strain_yy + strain_zz))
    str_yy = str_yy + time_step * (p_modulus * strain_yy + lame_lambda * (strain_xx + strain_zz))
    str_zz = str_zz + time_step * (p_modulus * strain_zz + lame_lambda * (strain_xx + strain_yy))
    str_xy = str_xy + time_step * shear_modulus * (forward_diff(vel_x, 2) + vy_ahead_x)
    str_xz = str_xz + time_step * shear_modulus * (vx_ahead_z + vz_ahead_x)
    str_yz = str_yz + time_step * shear_modulus * (vy_ahead_z + forward_diff(vel_z, 2))
    return [vel_x, vel_y, vel_z, str_xx, str_yy, str_zz, str_xy, str_xz, str_yz]


def leapfrog(fields, buoyancy, lame_lambda, shear_modulus):
    vel_x, vel_y, vel_z, str_xx, str_yy, str_zz, str_xy, str_xz, str_yz = fields
    stress_pad = with_halo(
        jnp.stack([str_xx, str_zz, str_xy, str_xz, str_yz]), (("horiz", 2), ("depth", 1)), 1
    )
    vel_x = vel_x + time_step * buoyancy * (
        ahead_x(stress_pad[0]) + backward_diff(str_xy, 2) + behind_z(stress_pad[3])
    )
    vel_y = vel_y + time_step * buoyancy * (
        behind_x(stress_pad[2]) + forward_diff(str_yy, 2) + behind_z(stress_pad[4])
    )
    vel_z = vel_z + time_step * buoyancy * (
        behind_x(stress_pad[3]) + backward_diff(str_yz, 2) + ahead_z(stress_pad[1])
    )
    velocity_pad = with_halo(jnp.stack([vel_x, vel_y, vel_z]), (("horiz", 2), ("depth", 1)), 1)
    return update_stresses(
        vel_x,
        vel_y,
        vel_z,
        str_xx,
        str_yy,
        str_zz,
        str_xy,
        str_xz,
        str_yz,
        behind_x(velocity_pad[0]),
        behind_z(velocity_pad[2]),
        ahead_z(velocity_pad[0]),
        ahead_x(velocity_pad[1]),
        ahead_z(velocity_pad[1]),
        ahead_x(velocity_pad[2]),
        lame_lambda,
        shear_modulus,
    )


def shards(
    adjoint_state,
    buoyancy,
    lame_lambda,
    shear_modulus,
    forward_field,
    traces,
    observed,
    pairs,
    patch_basis,
    patch_ids,
    slot_counts,
    owner_map,
):
    local_stations, local_blocks, samples = traces.shape
    bin_count = samples // 2
    tile_count = lax.axis_size("horiz")
    slab_count = lax.axis_size("depth")
    tile_index = lax.axis_index("horiz")
    depth_index = lax.axis_index("depth")
    stations = local_stations * tile_count
    group_items = local_blocks * bin_count
    items_dev = group_items // tile_count
    n_pairs = pairs.shape[0]
    x_cells = forward_field.shape[1]
    y_cells = forward_field.shape[2]
    sample_index = lax.iota(jnp.int32, samples)
    frequency = lax.iota(jnp.int32, bin_count) + 1
    phases = sample_index[:, None] * frequency[None, :] % samples
    angles = phases.astype(jnp.float32) * (2.0 * math.pi / samples)
    fourier_table = jnp.concatenate([jnp.cos(angles), -jnp.sin(angles)], axis=1) / math.sqrt(
        samples
    )
    spectra = jnp.einsum("sbt,tm->mbs", traces, fourier_table, precision=precise_mode)
    spectra = spectra.reshape(2, tile_count, items_dev, local_stations)
    first_station = pairs[:, 0]
    second_station = pairs[:, 1]
    received_block = lax.all_to_all(spectra, "horiz", split_axis=1, concat_axis=3, tiled=True)[:, 0]
    first_spec = jnp.take(received_block, first_station, axis=2)
    second_spec = jnp.take(received_block, second_station, axis=2)
    cross_real = first_spec[0] * second_spec[0] + first_spec[1] * second_spec[1]
    cross_imag = first_spec[0] * second_spec[1] - first_spec[1] * second_spec[0]
    cross = jnp.stack([cross_real, cross_imag])
    items_all = group_items * slab_count
    positions = (
        depth_index * group_items + tile_index * items_dev + lax.iota(jnp.int32, items_dev)
    ).astype(jnp.float32)
    weights = 1.0 + 2.0 * positions / (items_all - 1)
    deviation = cross - observed[0]
    pair_terms = jnp.sum(weights[None, :, None] * deviation * deviation, axis=(0, 1)) / (
        2.0 * items_all
    )
    all_terms = lax.psum(pair_terms, ("horiz", "depth"))
    total_all = jax.ops.segment_sum(all_terms, first_station, stations) + jax.ops.segment_sum(
        all_terms, second_station, stations
    )
    station_total = lax.dynamic_slice_in_dim(total_all, tile_index * local_stations, local_stations)
    unit_terms = jnp.ones((n_pairs,), jnp.float32)
    count_all = jax.ops.segment_sum(unit_terms, first_station, stations) + jax.ops.segment_sum(
        unit_terms, second_station, stations
    )
    station_count = lax.dynamic_slice_in_dim(count_all, tile_index * local_stations, local_stations)
    station_weight = station_total / jnp.maximum(station_count, 1.0)
    station_slot = lax.iota(jnp.int32, local_stations)
    onehot_x = ((station_slot % x_cells)[:, None] == lax.iota(jnp.int32, x_cells)[None, :]).astype(
        jnp.float32
    )
    onehot_y = (
        (53 * station_slot % y_cells)[:, None] == lax.iota(jnp.int32, y_cells)[None, :]
    ).astype(jnp.float32)
    deposit = jnp.dot((station_weight[:, None] * onehot_x).T, onehot_y, precision=precise_mode)
    surface = (depth_index == 0).astype(jnp.float32)
    fields = list(adjoint_state)
    fields[2] = fields[2].at[0].add(surface * deposit)
    for iteration in range(ITERS):
        fields = leapfrog(fields, buoyancy, lame_lambda, shear_modulus)
    adjoint_final = jnp.stack(fields)
    kernel = jnp.sum(fields[2] * forward_field, axis=0)
    slot_rows = jnp.dot(patch_basis, kernel, precision=precise_mode)
    n_slots = patch_ids.shape[1]
    n_patch = owner_map.shape[0]
    slot_used = lax.iota(jnp.int32, n_slots) < slot_counts[0]
    slot_ids = patch_ids[0]
    patch_order = lax.iota(jnp.int32, n_patch)
    same_owner = owner_map[:, None] == owner_map[None, :]
    earlier = patch_order[None, :] < patch_order[:, None]
    patch_rank = jnp.sum((same_owner & earlier).astype(jnp.int32), axis=1)
    rank_slots = lax.iota(jnp.int32, OWN_CAP)
    target = owner_map[slot_ids]
    dest_hot = (
        (target[:, None] == lax.iota(jnp.int32, tile_count)[None, :]) & slot_used[:, None]
    ).astype(jnp.int32)
    running = jnp.cumsum(dest_hot, axis=0) - 1
    position = jnp.sum(dest_hot * running, axis=1)
    buffer_index = target * CAP + position
    selector = (
        lax.iota(jnp.int32, tile_count * CAP)[:, None] == buffer_index[None, :]
    ) & slot_used[None, :]
    send_rows = jnp.dot(selector.astype(jnp.float32), slot_rows, precision=precise_mode).reshape(
        tile_count, CAP, y_cells
    )
    send_ids = jnp.sum(jnp.where(selector, slot_ids[None, :], 0), axis=1).reshape(tile_count, CAP)
    got_rows, got_ids = (
        lax.all_to_all(send_rows, "horiz", split_axis=0, concat_axis=0, tiled=True),
        lax.all_to_all(send_ids, "horiz", split_axis=0, concat_axis=0, tiled=True),
    )
    got_rows = got_rows.reshape(tile_count * CAP, y_cells)
    got_ids = got_ids.reshape(tile_count * CAP)
    placing = (
        (patch_rank[got_ids][None, :] == rank_slots[:, None])
        & (owner_map[got_ids] == tile_index)[None, :]
    ).astype(jnp.float32)
    patch_grad = jnp.dot(placing, got_rows, precision=precise_mode)
    return (adjoint_final, cross[None], patch_grad[None])


LEV, XC, YC, STN, BLK, FREQ = 8, 16, 128, 32, 8, 8
VX, VY, VZ, SXX, SYY, SZZ, SXY, SXZ, SYZ, BUO, LAM, MU = range(12)
EXT_X = XC + 8
FIRST = 5
CHUNKS = 6
EARLY = 3
WIDE = 2
V_LEVELS = 2
S_LEVELS = 2
ALL_VMEM = 67043328
SPARE = 2**11
MESH = pl.DeviceIdType.MESH


def split3(value):
    high = value.astype(jnp.bfloat16)
    rest = value - high.astype(jnp.float32)
    mid = rest.astype(jnp.bfloat16)
    low = (rest - mid.astype(jnp.float32)).astype(jnp.bfloat16)
    return high, mid, low


def dot32(a, b, dims):
    return lax.dot_general(
        a, b, (dims, ((), ())), precision=precise_mode, preferred_element_type=jnp.float32
    )


def roll_x(f, up):
    return pltpu.roll(f, EXT_X - 1 if up else 1, 0)


def velocity_levels(ext, mats, first, count):
    lane = lax.broadcasted_iota(jnp.int32, (EXT_X, YC), 1)

    def ahead_y(f):
        return jnp.where(lane == YC - 1, 0.0, pltpu.roll(f, YC - 1, 1)) - f

    def behind_y(f):
        return f - jnp.where(lane == 0, 0.0, pltpu.roll(f, 1, 1))

    results = []
    for i in range(count):
        z = first + i
        sxy = ext[SXY, z]
        sxz = ext[SXZ, z]
        syz = ext[SYZ, z]
        sxx = ext[SXX, z]
        scale = time_step * mats[BUO, z]
        vx = ext[VX, z] + scale * (
            (roll_x(sxx, True) - sxx) + behind_y(sxy) + (sxz - ext[SXZ, z - 1])
        )
        vy = ext[VY, z] + scale * (
            (sxy - roll_x(sxy, False)) + ahead_y(ext[SYY, z]) + (syz - ext[SYZ, z - 1])
        )
        vz = ext[VZ, z] + scale * (
            (sxz - roll_x(sxz, False)) + behind_y(syz) + (ext[SZZ, z + 1] - ext[SZZ, z])
        )
        results.append((vx, vy, vz))
    for i in range(count):
        for k, value in zip((VX, VY, VZ), results[i]):
            ext[k, first + i] = value


def stress_levels(ext, mats, first, count):
    lane = lax.broadcasted_iota(jnp.int32, (EXT_X, YC), 1)

    def ahead_y(f):
        return jnp.where(lane == YC - 1, 0.0, pltpu.roll(f, YC - 1, 1)) - f

    def behind_y(f):
        return f - jnp.where(lane == 0, 0.0, pltpu.roll(f, 1, 1))

    results = []
    for i in range(count):
        z = first + i
        vx = ext[VX, z]
        vy = ext[VY, z]
        vz = ext[VZ, z]
        lam = time_step * mats[LAM, z]
        mu = time_step * mats[MU, z]
        exx = vx - roll_x(vx, False)
        eyy = behind_y(vy)
        ezz = vz - ext[VZ, z - 1]
        p_mod = lam + 2.0 * mu
        sxx = ext[SXX, z] + (p_mod * exx + lam * (eyy + ezz))
        syy = ext[SYY, z] + (p_mod * eyy + lam * (exx + ezz))
        szz = ext[SZZ, z] + (p_mod * ezz + lam * (exx + eyy))
        sxy = ext[SXY, z] + mu * (ahead_y(vx) + (roll_x(vy, True) - vy))
        sxz = ext[SXZ, z] + mu * ((ext[VX, z + 1] - vx) + (roll_x(vz, True) - vz))
        syz = ext[SYZ, z] + mu * ((ext[VY, z + 1] - vy) + ahead_y(vz))
        results.append((sxx, syy, szz, sxy, sxz, syz))
    for i in range(count):
        for k, value in zip((SXX, SYY, SZZ, SXY, SXZ, SYZ), results[i]):
            ext[k, first + i] = value


def in_trips(levels, ext, first, total, count):
    def body(i, carry):
        levels(ext, ext, first + count * i, count)
        return carry

    trips, rest = divmod(total, count)
    if trips:
        lax.fori_loop(0, trips, body, 0)
    if rest:
        levels(ext, ext, first + count * trips, rest)


def fused_kernel(
    tiles,
    slabs,
    state_ref,
    buo_ref,
    lam_ref,
    mu_ref,
    forward_hbm,
    traces_hbm,
    observed_hbm,
    pairs_hbm,
    basis_hbm,
    ids_hbm,
    counts_hbm,
    owner_hbm,
    table_hbm,
    final_out,
    cross_out,
    rows_in,
    ext,
    cross_ref,
    forward_ref,
    traces_ref,
    observed_ref,
    pairs_ref,
    basis_ref,
    ids_ref,
    counts_ref,
    owner_ref,
    table_ref,
    pack_r,
    pack_l,
    halo_r,
    halo_l,
    spec_out,
    spec_in,
    left_rows,
    right_rows,
    part,
    parts,
    added,
    rows_out,
    local_sem,
    spec_send,
    spec_recv,
    slab_send,
    slab_recv,
    side_send,
    side_recv,
    corner_send,
    corner_recv,
    part_send,
    part_recv,
    row_send,
    row_recv,
    far_sem,
):
    me = lax.axis_index("horiz")
    depth = lax.axis_index("depth")
    n_pairs = pairs_ref.shape[1]
    own = pl.ds(FIRST, LEV)
    arrays = ((0, 9, state_ref), (9, 1, buo_ref), (10, 1, lam_ref), (11, 1, mu_ref))
    pair_rows = tiles // WIDE
    row_z, row_y = me // WIDE, lax.rem(me, WIDE)

    barrier = pltpu.get_barrier_semaphore()
    for d in range(1, slabs):
        other = {"depth": lax.rem(depth + d, slabs)}
        pl.semaphore_signal(barrier, inc=1, device_id=other, device_id_type=MESH)
    for k in range(1, WIDE):
        other = {"horiz": row_z * WIDE + lax.rem(row_y + k, WIDE)}
        pl.semaphore_signal(barrier, inc=1, device_id=other, device_id_type=MESH)

    def near_rows(run):
        for step in (-1, 1):

            @pl.when((row_z + step >= 0) & (row_z + step < pair_rows))
            def _():
                run(step)

    def greet(step):
        for k in range(WIDE):
            other = {"horiz": (row_z + step) * WIDE + k}
            pl.semaphore_signal(barrier, inc=1, device_id=other, device_id_type=MESH)

    near_rows(greet)

    smalls = (
        (traces_hbm, traces_ref),
        (table_hbm, table_ref),
        (pairs_hbm, pairs_ref),
        (basis_hbm, basis_ref),
        (ids_hbm, ids_ref),
        (counts_hbm, counts_ref),
        (owner_hbm, owner_ref),
        (observed_hbm, observed_ref),
        (forward_hbm, forward_ref),
    )
    small_in = [
        pltpu.make_async_copy(src, dst, local_sem.at[4 + n]) for n, (src, dst) in enumerate(smalls)
    ]
    locals_in = [
        pltpu.make_async_copy(
            src, ext.at[pl.ds(start, count), own, pl.ds(0, XC)], local_sem.at[n]
        )
        for n, (start, count, src) in enumerate(arrays)
    ]
    for copy in small_in[:2] + locals_in + small_in[2:]:
        copy.start()

    row = lax.broadcasted_iota(jnp.int32, (8, YC), 0)
    lower = row < 4
    for copy in small_in[:2]:
        copy.wait()
    by_block = jnp.concatenate(
        [traces_ref[pl.ds(b, STN, stride=BLK), :] for b in range(BLK)], axis=0
    )
    spectra = dot32(table_ref[...], by_block, ((1,), (1,)))
    half = tiles * FREQ
    for t in range(tiles):
        for c in range(2):
            spec_out[t, pl.ds(c * FREQ, FREQ), :] = spectra[
                c * half + t * FREQ : c * half + (t + 1) * FREQ
            ]
    for copy in locals_in:
        copy.wait()

    def pack_one(a, carry):
        for j in range(LEV // 2):
            even, odd = FIRST + 2 * j, FIRST + 2 * j + 1
            pack_r[a, j] = jnp.where(
                lower, ext[a, even, pl.ds(0, 8)], pltpu.roll(ext[a, odd, pl.ds(0, 8)], 4, 0)
            )
            pack_l[a, j] = jnp.where(
                lower, pltpu.roll(ext[a, odd, pl.ds(8, 8)], 4, 0), ext[a, even, pl.ds(8, 8)]
            )
        return carry

    lax.fori_loop(0, 12, pack_one, 0)

    mid_pairs = pl.ds(2, LEV // 2)

    def side_copy(n, c):
        source, target, step = ((pack_r, halo_r, -1), (pack_l, halo_l, 1))[n]
        some = pl.ds(c * 12 // CHUNKS, 12 // CHUNKS)
        return pltpu.make_async_remote_copy(
            src_ref=source.at[some],
            dst_ref=target.at[some, mid_pairs],
            send_sem=side_send.at[n],
            recv_sem=side_recv.at[n, c],
            device_id={"horiz": me + step},
            device_id_type=MESH,
        )

    def slab_copy(n, m):
        start, count, src = arrays[m]
        levels = pl.ds(0, 4) if n == 0 else pl.ds(LEV - 4, 4)
        source = src.at[:, levels]
        target = ext.at[
            pl.ds(start, count), pl.ds(FIRST + LEV if n == 0 else FIRST - 4, 4), pl.ds(0, XC)
        ]
        return pltpu.make_async_remote_copy(
            src_ref=source,
            dst_ref=target,
            send_sem=slab_send.at[n],
            recv_sem=slab_recv.at[n],
            device_id={"depth": depth + (-1 if n == 0 else 1)},
            device_id_type=MESH,
        )

    def corner_copy(n, m, c):
        buffer = (halo_r, halo_l)[m]
        some = pl.ds(c * 12 // CHUNKS, 12 // CHUNKS)
        return pltpu.make_async_remote_copy(
            src_ref=buffer.at[some, pl.ds(2 if n == 0 else 4, 2)],
            dst_ref=buffer.at[some, pl.ds(6 if n == 0 else 0, 2)],
            send_sem=corner_send.at[n, m],
            recv_sem=corner_recv.at[n, m],
            device_id={"depth": depth + (-1 if n == 0 else 1)},
            device_id_type=MESH,
        )

    def whole(src, dst, send, recv):
        return pltpu.make_async_remote_copy(
            src_ref=src,
            dst_ref=dst,
            send_sem=send,
            recv_sem=recv,
            device_id={"horiz": me},
            device_id_type=MESH,
        )

    def sides(n):
        source, target = ((pack_r, halo_r), (pack_l, halo_l))[n]
        return whole(source, target.at[:, mid_pairs], side_send.at[n], side_recv.at[n, 0])

    def slab(n):
        levels = ext.at[
            :, pl.ds(FIRST + LEV if n == 0 else FIRST - 4, 4), pl.ds(0, XC)
        ]
        return whole(levels, levels, slab_send.at[n], slab_recv.at[n])

    def corners(n, m):
        buffer = (halo_r, halo_l)[m]
        return whole(
            buffer.at[:, pl.ds(2 if n == 0 else 4, 2)],
            buffer.at[:, pl.ds(6 if n == 0 else 0, 2)],
            corner_send.at[n, m],
            corner_recv.at[n, m],
        )

    has_left, has_right = me > 0, me < tiles - 1
    has_up, has_down = depth > 0, depth < slabs - 1

    def side_start(c):
        @pl.when(has_left)
        def _():
            side_copy(0, c).start()

        @pl.when(has_right)
        def _():
            side_copy(1, c).start()

    def spec_copy(peer, source):
        return pltpu.make_async_remote_copy(
            src_ref=spec_out.at[peer],
            dst_ref=spec_in.at[source],
            send_sem=spec_send,
            recv_sem=spec_recv,
            device_id={"horiz": peer},
            device_id_type=MESH,
        )

    def far_signal(step, stage):
        pl.semaphore_signal(
            far_sem.at[(step + 1) // 2, stage],
            inc=1,
            device_id={"horiz": me + step * WIDE},
            device_id_type=MESH,
        )

    def spec_row(distance):
        for step in (-1, 1):
            there = row_z + step * distance

            @pl.when((there >= 0) & (there < pair_rows))
            def _():
                for k in range(WIDE):
                    spec_copy(there * WIDE + k, me).start()

    pl.semaphore_wait(
        barrier,
        slabs
        - 1
        + WIDE
        - 1
        + jnp.where(row_z > 0, WIDE, 0)
        + jnp.where(row_z < pair_rows - 1, WIDE, 0),
    )
    for step in (-1, 1):

        @pl.when(
            (row_z - step >= 0)
            & (row_z - step < pair_rows)
            & (row_z + step >= 0)
            & (row_z + step < pair_rows)
        )
        def _():
            far_signal(step, 0)

    for c in range(EARLY):
        side_start(c)

    @pl.when(has_up)
    def _():
        for m in range(4):
            slab_copy(0, m).start()

    @pl.when(has_down)
    def _():
        for m in range(4):
            slab_copy(1, m).start()

    for k in range(1, WIDE):
        spec_copy(row_z * WIDE + lax.rem(row_y + k, WIDE), me).start()
    spec_row(1)
    for distance in range(2, pair_rows):
        for step in (-1, 1):
            source = row_z - step * distance
            after = row_z + step

            @pl.when((source >= 0) & (source < pair_rows))
            def _():
                pl.semaphore_wait(far_sem.at[(step + 1) // 2, distance - 2], 1)
                if distance < pair_rows - 1:

                    @pl.when((after >= 0) & (after < pair_rows))
                    def _():
                        far_signal(step, distance - 1)

        spec_row(distance)
    for c in range(EARLY, CHUNKS):
        side_start(c)
    spec_in[me] = spec_out[me]

    def clear_levels(first):
        def clear(a, carry):
            for i in range(4):
                ext[a, first + i] = jnp.zeros((EXT_X, YC), jnp.float32)
            return carry

        lax.fori_loop(0, 12, clear, 0)

    def clear_pairs(buffer, first, count):
        def clear(a, carry):
            for i in range(count):
                buffer[a, first + i] = jnp.zeros((8, YC), jnp.float32)
            return carry

        lax.fori_loop(0, 12, clear, 0)

    @pl.when(jnp.logical_not(has_up))
    def _():
        clear_levels(FIRST - 4)
        clear_pairs(halo_r, 0, 2)
        clear_pairs(halo_l, 0, 2)

    @pl.when(jnp.logical_not(has_down))
    def _():
        clear_levels(FIRST + LEV)
        clear_pairs(halo_r, 6, 2)
        clear_pairs(halo_l, 6, 2)

    @pl.when(jnp.logical_not(has_right))
    def _():
        clear_pairs(halo_r, 2, 4)

    @pl.when(jnp.logical_not(has_left))
    def _():
        clear_pairs(halo_l, 2, 4)

    def clear_ends(a, carry):
        ext[a, 0] = jnp.zeros((EXT_X, YC), jnp.float32)
        ext[a, 17] = jnp.zeros((EXT_X, YC), jnp.float32)
        return carry

    lax.fori_loop(0, 12, clear_ends, 0)

    def clear_added(a, carry):
        for i in range(ITERS + 3):
            added[a, FIRST - 1 + i] = jnp.zeros((EXT_X, YC), jnp.float32)
        return carry

    @pl.when(depth == 0)
    def _():
        lax.fori_loop(0, 9, clear_added, 0)

    for copy in small_in[2:7]:
        copy.wait()
    first_pair = pairs_ref[pl.ds(0, 1), :]
    second_pair = pairs_ref[pl.ds(1, 1), :]
    stations = tiles * STN
    station = lax.broadcasted_iota(jnp.int32, (stations, n_pairs), 0)
    hot_first = (station == first_pair).astype(jnp.float32).astype(jnp.bfloat16)
    hot_second = (station == second_pair).astype(jnp.float32).astype(jnp.bfloat16)
    n_patch = owner_ref.shape[1]
    n_slots = ids_ref.shape[1]
    owner_row = owner_ref[...]
    up_iota = lax.broadcasted_iota(jnp.int32, (n_patch, n_patch), 0)
    across = lax.broadcasted_iota(jnp.int32, (n_patch, n_patch), 1)
    owner_wide = jnp.broadcast_to(owner_row, (n_patch, n_patch))
    owner_col = jnp.sum(jnp.where(up_iota == across, owner_wide, 0), axis=1, keepdims=True)
    rank_row = jnp.sum(
        jnp.where((owner_col == owner_wide) & (up_iota < across), 1, 0), axis=0, keepdims=True
    )
    target_row = owner_row * OWN_CAP + rank_row
    out_rows = tiles * OWN_CAP
    place = (
        lax.broadcasted_iota(jnp.int32, (out_rows, n_patch), 0) == target_row
    ).astype(jnp.float32)
    slot = lax.broadcasted_iota(jnp.int32, (n_patch, n_slots), 1)
    patch = lax.broadcasted_iota(jnp.int32, (n_patch, n_slots), 0)
    named = ((patch == ids_ref[...]) & (slot < counts_ref[...])).astype(jnp.float32)
    slot_place = dot32(place, named, ((1,), (0,)))
    row_basis = dot32(slot_place, basis_ref[...], ((1,), (0,)))

    def relay(first, last):
        for c in range(first, last):

            @pl.when(has_left)
            def _():
                side_copy(1, c).wait_recv()

            @pl.when(has_right)
            def _():
                side_copy(0, c).wait_recv()

            @pl.when(has_up)
            def _():
                for m in range(2):
                    corner_copy(0, m, c).start()

            @pl.when(has_down)
            def _():
                for m in range(2):
                    corner_copy(1, m, c).start()

    relay(0, EARLY)
    others = pl.ds(0, tiles - 1)
    whole(spec_out.at[others], spec_in.at[others], spec_send, spec_recv).wait_recv()
    small_in[7].wait()
    for b in range(BLK):
        wide = jnp.concatenate(
            [spec_in[t][:, b * STN : (b + 1) * STN] for t in range(tiles)], axis=1
        )
        left_rows[pl.ds(b * 2 * FREQ, 2 * FREQ), :] = wide[:, :128]
        right_rows[pl.ds(b * 2 * FREQ, 2 * FREQ), :] = wide[:, 128:]
    ordered = jnp.concatenate(
        [
            jnp.concatenate(
                [r[pl.ds(cf, BLK, stride=2 * FREQ), :] for cf in range(2 * FREQ)], axis=0
            )
            for r in (left_rows, right_rows)
        ],
        axis=1,
    )
    pieces = split3(ordered)

    def gather(hot):
        return sum(
            lax.dot_general(
                piece, hot, (((1,), (0,)), ((), ())), preferred_element_type=jnp.float32
            )
            for piece in pieces[::-1]
        )

    first_spec = gather(hot_first)
    second_spec = gather(hot_second)
    items = FREQ * BLK
    f_re, f_im = first_spec[:items], first_spec[items:]
    s_re, s_im = second_spec[:items], second_spec[items:]
    cross_re = f_re * s_re + f_im * s_im
    cross_im = f_re * s_im - f_im * s_re
    items_all = items * tiles * slabs
    item = lax.broadcasted_iota(jnp.int32, (items, 1), 0) + (depth * tiles + me) * items
    weight = 1.0 + 2.0 * item.astype(jnp.float32) / (items_all - 1)
    dev_re = cross_re - observed_ref[0, 0]
    dev_im = cross_im - observed_ref[0, 1]
    terms = weight * (dev_re * dev_re + dev_im * dev_im)
    part[...] = jnp.sum(terms, axis=0, keepdims=True)

    def part_copy(d, k):
        slot = d * tiles + me
        return pltpu.make_async_remote_copy(
            src_ref=part,
            dst_ref=parts.at[slot],
            send_sem=part_send,
            recv_sem=part_recv,
            device_id={"horiz": lax.rem(me + k, tiles), "depth": 0},
            device_id_type=MESH,
        )

    for k in range(1, tiles):
        part_copy(depth, k).start()

    @pl.when(depth > 0)
    def _():
        part_copy(depth, 0).start()

    cross_ref[0, 0] = cross_re
    cross_ref[0, 1] = cross_im
    cross_copy = pltpu.make_async_copy(cross_ref, cross_out, local_sem.at[13])
    cross_copy.start()

    relay(EARLY, CHUNKS)

    def unpack(first, count):
        def unpack_one(a, carry):
            for j in range(first, first + count):
                r, l = halo_r[a, j], halo_l[a, j]
                ext[a, 1 + 2 * j, pl.ds(XC, 8)] = jnp.where(lower, r, l)
                ext[a, 2 + 2 * j, pl.ds(XC, 8)] = pltpu.roll(jnp.where(lower, l, r), 4, 0)
            return carry

        lax.fori_loop(0, 12, unpack_one, 0)

    unpack(2, 4)

    @pl.when(has_up)
    def _():
        slab(1).wait_recv()
        for m in range(2):
            corners(1, m).wait_recv()

    @pl.when(has_down)
    def _():
        slab(0).wait_recv()
        for m in range(2):
            corners(0, m).wait_recv()

    unpack(0, 2)
    unpack(6, 2)

    for n in range(ITERS):
        in_trips(velocity_levels, ext, 1 + n, 16 - 2 * n, V_LEVELS)
        in_trips(stress_levels, ext, 2 + n, 14 - 2 * n, S_LEVELS)

    @pl.when(depth == 0)
    def _():
        senders = parts.at[pl.ds(0, tiles * slabs - 1)]
        whole(senders, senders, part_send, part_recv).wait_recv()
        parts[me] = part[...]
        total = parts[0]
        for t in range(1, tiles * slabs):
            total = total + parts[t]
        terms = total / (2.0 * items_all)
        ext_row = lax.broadcasted_iota(jnp.int32, (EXT_X, 1), 0)
        x = me * XC + jnp.where(ext_row < XC + 4, ext_row, ext_row - EXT_X)
        x_pos = x + XC
        tile = x_pos // XC - 1
        in_tile = x_pos - (tile + 1) * XC
        lane = lax.broadcasted_iota(jnp.int32, (EXT_X, YC), 1)
        deposit = jnp.zeros((EXT_X, YC), jnp.float32)
        for turn in range(STN // XC):
            within = in_tile + turn * XC
            index = tile * STN + within
            hits = (index == first_pair).astype(jnp.float32) + (index == second_pair).astype(
                jnp.float32
            )
            sums = jnp.sum(hits * terms, axis=1, keepdims=True)
            number = jnp.sum(hits, axis=1, keepdims=True)
            value = sums / jnp.maximum(number, 1.0)
            deposit = deposit + jnp.where(lane == lax.rem(53 * within, YC), value, 0.0)
        added[VZ, FIRST] = deposit
        for n in range(ITERS):
            if n:
                for z in range(0, n + 1, 2):
                    velocity_levels(added, ext, FIRST + z, min(2, n + 1 - z))
            for z in range(0, n + 2, 2):
                stress_levels(added, ext, FIRST + z, min(2, n + 2 - z))

        def add_one(a, carry):
            for i in range(ITERS + 1):
                ext[a, FIRST + i, pl.ds(0, XC)] += added[a, FIRST + i, pl.ds(0, XC)]
            return carry

        lax.fori_loop(0, 9, add_one, 0)

    final = pltpu.make_async_copy(
        ext.at[pl.ds(0, 9), own, pl.ds(0, XC)], final_out, local_sem.at[14]
    )
    final.start()
    small_in[8].wait()
    weighted = sum(ext[VZ, FIRST + i, pl.ds(0, XC)] * forward_ref[i] for i in range(LEV))
    rows = dot32(row_basis, weighted, ((1,), (0,)))
    for t in range(tiles):
        rows_out[t] = rows[t * OWN_CAP : (t + 1) * OWN_CAP]
    row_copies = []
    for k in range(1, tiles):
        peer = lax.rem(me + k, tiles)
        row_copies.append(
            pltpu.make_async_remote_copy(
                src_ref=rows_out.at[peer],
                dst_ref=rows_in.at[me],
                send_sem=row_send,
                recv_sem=row_recv,
                device_id={"horiz": peer},
                device_id_type=MESH,
            )
        )
    for copy in row_copies:
        copy.start()
    own_rows = pltpu.make_async_copy(rows_out.at[me], rows_in.at[me], local_sem.at[15])
    own_rows.start()

    whole(spec_out.at[others], spec_in.at[others], spec_send, spec_recv).wait_send()

    @pl.when(has_left)
    def _():
        sides(0).wait_send()

    @pl.when(has_right)
    def _():
        sides(1).wait_send()

    @pl.when(has_up)
    def _():
        slab(0).wait_send()
        for m in range(2):
            corners(0, m).wait_send()

    @pl.when(has_down)
    def _():
        slab(1).wait_send()
        for m in range(2):
            corners(1, m).wait_send()

    @pl.when(depth == 0)
    def _():
        sent = parts.at[pl.ds(0, tiles - 1)]
        whole(sent, sent, part_send, part_recv).wait_send()

    @pl.when(depth > 0)
    def _():
        sent = parts.at[pl.ds(0, tiles)]
        whole(sent, sent, part_send, part_recv).wait_send()

    all_rows = whole(rows_out.at[others], rows_in.at[others], row_send, row_recv)
    all_rows.wait_recv()
    all_rows.wait_send()
    own_rows.wait()
    cross_copy.wait()
    final.wait()


def hand_out_kernel(state, cross, rows, state_ref, cross_ref, grad_ref, grad, out_sem):
    writes = [
        pltpu.make_async_copy(src, dst, out_sem.at[n])
        for n, (src, dst) in enumerate(
            ((state, state_ref), (cross, cross_ref), (grad, grad_ref))
        )
    ]
    writes[0].start()
    writes[1].start()
    grad[0] = sum(rows[t] for t in range(rows.shape[0]))
    writes[2].start()
    for write in writes:
        write.wait()


def hand_out(state, cross, rows):
    anywhere = pl.BlockSpec(memory_space=pl.ANY)
    vmem = pl.BlockSpec(memory_space=pltpu.VMEM)
    grad = jax.ShapeDtypeStruct((1,) + rows.shape[1:], rows.dtype)
    return pl.pallas_call(
        hand_out_kernel,
        out_shape=(
            jax.ShapeDtypeStruct(state.shape, state.dtype),
            jax.ShapeDtypeStruct(cross.shape, cross.dtype),
            grad,
        ),
        in_specs=[anywhere, anywhere, vmem],
        out_specs=(anywhere,) * 3,
        scratch_shapes=[
            pltpu.VMEM(grad.shape, grad.dtype),
            pltpu.SemaphoreType.DMA((3,)),
        ],
        compiler_params=pltpu.CompilerParams(vmem_limit_bytes=2**20),
    )(state, cross, rows)


def fused_shards(
    adjoint_state,
    buoyancy,
    lame_lambda,
    shear_modulus,
    forward_field,
    traces,
    observed,
    pairs,
    patch_basis,
    patch_ids,
    slot_counts,
    owner_map,
):
    tiles, slabs = lax.axis_size("horiz"), lax.axis_size("depth")
    samples = traces.shape[2]
    n_pairs = pairs.shape[0]
    bins = samples // 2
    phases = np.outer(np.arange(1, bins + 1), np.arange(samples)) % samples
    angles = phases * (2.0 * math.pi / samples)
    table = np.concatenate([np.cos(angles), -np.sin(angles)], axis=0) / math.sqrt(samples)
    anywhere = pl.BlockSpec(memory_space=pl.ANY)
    f32 = jnp.float32
    dma = pltpu.SemaphoreType.DMA
    kept = 4 * (
        math.prod(adjoint_state.shape) + math.prod(observed.shape) + tiles * OWN_CAP * YC
    )
    return pl.pallas_call(
        functools.partial(fused_kernel, tiles, slabs),
        out_shape=(
            pltpu.VMEM(adjoint_state.shape, f32),
            pltpu.VMEM(observed.shape, f32),
            pltpu.VMEM((tiles, OWN_CAP, YC), f32),
        ),
        in_specs=[anywhere] * 13,
        out_specs=(anywhere, anywhere, anywhere),
        scratch_shapes=[
            pltpu.VMEM((12, LEV + 10, EXT_X, YC), f32),
            pltpu.VMEM(observed.shape, f32),
            pltpu.VMEM(forward_field.shape, f32),
            pltpu.VMEM((STN * BLK, samples), f32),
            pltpu.VMEM(observed.shape, f32),
            pltpu.VMEM((2, n_pairs), jnp.int32),
            pltpu.VMEM(patch_basis.shape, f32),
            pltpu.VMEM(patch_ids.shape, jnp.int32),
            pltpu.VMEM((1, 1), jnp.int32),
            pltpu.VMEM((1, owner_map.shape[0]), jnp.int32),
            pltpu.VMEM(table.shape, f32),
            pltpu.VMEM((12, 4, 8, YC), f32),
            pltpu.VMEM((12, 4, 8, YC), f32),
            pltpu.VMEM((12, 8, 8, YC), f32),
            pltpu.VMEM((12, 8, 8, YC), f32),
            pltpu.VMEM((tiles, 2 * FREQ, BLK * STN), f32),
            pltpu.VMEM((tiles, 2 * FREQ, BLK * STN), f32),
            pltpu.VMEM((2 * FREQ * BLK, 128), f32),
            pltpu.VMEM((2 * FREQ * BLK, 128), f32),
            pltpu.VMEM((1, n_pairs), f32),
            pltpu.VMEM((tiles * slabs, 1, n_pairs), f32),
            pltpu.VMEM((9, FIRST + ITERS + 2, EXT_X, YC), f32),
            pltpu.VMEM((tiles, OWN_CAP, YC), f32),
            dma((16,)),
            pltpu.SemaphoreType.DMA(()),
            pltpu.SemaphoreType.DMA(()),
            dma((2,)),
            dma((2,)),
            dma((2,)),
            dma((2, CHUNKS)),
            dma((2, 2)),
            dma((2, 2)),
            pltpu.SemaphoreType.DMA(()),
            pltpu.SemaphoreType.DMA(()),
            pltpu.SemaphoreType.DMA(()),
            pltpu.SemaphoreType.DMA(()),
            pltpu.SemaphoreType.REGULAR((2, max(tiles // WIDE - 2, 1))),
        ],
        compiler_params=pltpu.CompilerParams(
            collective_id=0, has_side_effects=True, vmem_limit_bytes=ALL_VMEM - kept - SPARE
        ),
    )(
        adjoint_state,
        buoyancy[None],
        lame_lambda[None],
        shear_modulus[None],
        forward_field,
        traces.reshape(-1, samples),
        observed,
        pairs.T,
        patch_basis,
        patch_ids,
        slot_counts.reshape(1, 1),
        owner_map.reshape(1, -1),
        jnp.asarray(table, f32),
    )


def fits_fused(tiles, slabs, state, traces, pairs):
    return (
        state[1:] == (LEV, XC, YC)
        and traces == (STN, BLK, 128)
        and tiles * FREQ == 64
        and slabs > 1
        and pairs[0] % 128 == 0
    )


def local_program(*args):
    tiles, slabs = lax.axis_size("horiz"), lax.axis_size("depth")
    if fits_fused(tiles, slabs, args[0].shape, args[5].shape, args[7].shape):
        return hand_out(*fused_shards(*args))
    return shards(*args)


def solution(mesh):
    return jax.shard_map(
        local_program,
        mesh=mesh,
        in_specs=(
            P(None, "depth", "horiz", None),
            P("depth", "horiz", None),
            P("depth", "horiz", None),
            P("depth", "horiz", None),
            P("depth", "horiz", None),
            P("horiz", "depth", None),
            P("depth", None, "horiz", None),
            P(),
            P(None, "horiz"),
            P("horiz", None),
            P("horiz"),
            P(),
        ),
        out_specs=(
            P(None, "depth", "horiz", None),
            P("depth", None, "horiz", None),
            P("depth", "horiz", None),
        ),
        check_vma=False,
    )
```

```python
import functools
import math

import jax
import jax.numpy as jnp
import numpy as np
from jax import lax
from jax.experimental import pallas as pl
from jax.experimental.pallas import tpu as pltpu
from jax.sharding import PartitionSpec as P

ITERS = 4
CAP = 2
OWN_CAP = 8


time_step = 0.25
precise_mode = lax.Precision.HIGHEST


def with_halo(cells, sides, width):
    for axis, dim in sides:
        count = lax.axis_size(axis)
        ends = count - 1
        head = lax.slice_in_dim(cells, 0, width, axis=dim)
        tail = lax.slice_in_dim(cells, cells.shape[dim] - width, cells.shape[dim], axis=dim)
        cells = jnp.concatenate(
            [
                lax.ppermute(tail, axis, [(i, (i + 1) % count) for i in range(ends)]),
                cells,
                lax.ppermute(head, axis, [((i + 1) % count, i) for i in range(ends)]),
            ],
            axis=dim,
        )
    return cells


def forward_diff(field, along):
    extent = field.shape[along]
    ahead = jnp.concatenate(
        [
            lax.slice_in_dim(field, 1, extent, axis=along),
            jnp.zeros_like(lax.slice_in_dim(field, 0, 1, axis=along)),
        ],
        axis=along,
    )
    return ahead - field


def backward_diff(field, along):
    extent = field.shape[along]
    behind = jnp.concatenate(
        [
            jnp.zeros_like(lax.slice_in_dim(field, 0, 1, axis=along)),
            lax.slice_in_dim(field, 0, extent - 1, axis=along),
        ],
        axis=along,
    )
    return field - behind


def ahead_z(padded):
    return padded[2:, 1:-1] - padded[1:-1, 1:-1]


def behind_z(padded):
    return padded[1:-1, 1:-1] - padded[:-2, 1:-1]


def ahead_x(padded):
    return padded[1:-1, 2:] - padded[1:-1, 1:-1]


def behind_x(padded):
    return padded[1:-1, 1:-1] - padded[1:-1, :-2]


def update_stresses(
    vel_x,
    vel_y,
    vel_z,
    str_xx,
    str_yy,
    str_zz,
    str_xy,
    str_xz,
    str_yz,
    strain_xx,
    strain_zz,
    vx_ahead_z,
    vy_ahead_x,
    vy_ahead_z,
    vz_ahead_x,
    lame_lambda,
    shear_modulus,
):
    strain_yy = backward_diff(vel_y, 2)
    p_modulus = lame_lambda + 2.0 * shear_modulus
    str_xx = str_xx + time_step * (p_modulus * strain_xx + lame_lambda * (strain_yy + strain_zz))
    str_yy = str_yy + time_step * (p_modulus * strain_yy + lame_lambda * (strain_xx + strain_zz))
    str_zz = str_zz + time_step * (p_modulus * strain_zz + lame_lambda * (strain_xx + strain_yy))
    str_xy = str_xy + time_step * shear_modulus * (forward_diff(vel_x, 2) + vy_ahead_x)
    str_xz = str_xz + time_step * shear_modulus * (vx_ahead_z + vz_ahead_x)
    str_yz = str_yz + time_step * shear_modulus * (vy_ahead_z + forward_diff(vel_z, 2))
    return [vel_x, vel_y, vel_z, str_xx, str_yy, str_zz, str_xy, str_xz, str_yz]


def leapfrog(fields, buoyancy, lame_lambda, shear_modulus):
    vel_x, vel_y, vel_z, str_xx, str_yy, str_zz, str_xy, str_xz, str_yz = fields
    stress_pad = with_halo(
        jnp.stack([str_xx, str_zz, str_xy, str_xz, str_yz]), (("horiz", 2), ("depth", 1)), 1
    )
    vel_x = vel_x + time_step * buoyancy * (
        ahead_x(stress_pad[0]) + backward_diff(str_xy, 2) + behind_z(stress_pad[3])
    )
    vel_y = vel_y + time_step * buoyancy * (
        behind_x(stress_pad[2]) + forward_diff(str_yy, 2) + behind_z(stress_pad[4])
    )
    vel_z = vel_z + time_step * buoyancy * (
        behind_x(stress_pad[3]) + backward_diff(str_yz, 2) + ahead_z(stress_pad[1])
    )
    velocity_pad = with_halo(jnp.stack([vel_x, vel_y, vel_z]), (("horiz", 2), ("depth", 1)), 1)
    return update_stresses(
        vel_x,
        vel_y,
        vel_z,
        str_xx,
        str_yy,
        str_zz,
        str_xy,
        str_xz,
        str_yz,
        behind_x(velocity_pad[0]),
        behind_z(velocity_pad[2]),
        ahead_z(velocity_pad[0]),
        ahead_x(velocity_pad[1]),
        ahead_z(velocity_pad[1]),
        ahead_x(velocity_pad[2]),
        lame_lambda,
        shear_modulus,
    )


def shards(
    adjoint_state,
    buoyancy,
    lame_lambda,
    shear_modulus,
    forward_field,
    traces,
    observed,
    pairs,
    patch_basis,
    patch_ids,
    slot_counts,
    owner_map,
):
    local_stations, local_blocks, samples = traces.shape
    bin_count = samples // 2
    tile_count = lax.axis_size("horiz")
    slab_count = lax.axis_size("depth")
    tile_index = lax.axis_index("horiz")
    depth_index = lax.axis_index("depth")
    stations = local_stations * tile_count
    group_items = local_blocks * bin_count
    items_dev = group_items // tile_count
    n_pairs = pairs.shape[0]
    x_cells = forward_field.shape[1]
    y_cells = forward_field.shape[2]
    sample_index = lax.iota(jnp.int32, samples)
    frequency = lax.iota(jnp.int32, bin_count) + 1
    phases = sample_index[:, None] * frequency[None, :] % samples
    angles = phases.astype(jnp.float32) * (2.0 * math.pi / samples)
    fourier_table = jnp.concatenate([jnp.cos(angles), -jnp.sin(angles)], axis=1) / math.sqrt(
        samples
    )
    spectra = jnp.einsum("sbt,tm->mbs", traces, fourier_table, precision=precise_mode)
    spectra = spectra.reshape(2, tile_count, items_dev, local_stations)
    first_station = pairs[:, 0]
    second_station = pairs[:, 1]
    received_block = lax.all_to_all(spectra, "horiz", split_axis=1, concat_axis=3, tiled=True)[:, 0]
    first_spec = jnp.take(received_block, first_station, axis=2)
    second_spec = jnp.take(received_block, second_station, axis=2)
    cross_real = first_spec[0] * second_spec[0] + first_spec[1] * second_spec[1]
    cross_imag = first_spec[0] * second_spec[1] - first_spec[1] * second_spec[0]
    cross = jnp.stack([cross_real, cross_imag])
    items_all = group_items * slab_count
    positions = (
        depth_index * group_items + tile_index * items_dev + lax.iota(jnp.int32, items_dev)
    ).astype(jnp.float32)
    weights = 1.0 + 2.0 * positions / (items_all - 1)
    deviation = cross - observed[0]
    pair_terms = jnp.sum(weights[None, :, None] * deviation * deviation, axis=(0, 1)) / (
        2.0 * items_all
    )
    all_terms = lax.psum(pair_terms, ("horiz", "depth"))
    total_all = jax.ops.segment_sum(all_terms, first_station, stations) + jax.ops.segment_sum(
        all_terms, second_station, stations
    )
    station_total = lax.dynamic_slice_in_dim(total_all, tile_index * local_stations, local_stations)
    unit_terms = jnp.ones((n_pairs,), jnp.float32)
    count_all = jax.ops.segment_sum(unit_terms, first_station, stations) + jax.ops.segment_sum(
        unit_terms, second_station, stations
    )
    station_count = lax.dynamic_slice_in_dim(count_all, tile_index * local_stations, local_stations)
    station_weight = station_total / jnp.maximum(station_count, 1.0)
    station_slot = lax.iota(jnp.int32, local_stations)
    onehot_x = ((station_slot % x_cells)[:, None] == lax.iota(jnp.int32, x_cells)[None, :]).astype(
        jnp.float32
    )
    onehot_y = (
        (53 * station_slot % y_cells)[:, None] == lax.iota(jnp.int32, y_cells)[None, :]
    ).astype(jnp.float32)
    deposit = jnp.dot((station_weight[:, None] * onehot_x).T, onehot_y, precision=precise_mode)
    surface = (depth_index == 0).astype(jnp.float32)
    fields = list(adjoint_state)
    fields[2] = fields[2].at[0].add(surface * deposit)
    for iteration in range(ITERS):
        fields = leapfrog(fields, buoyancy, lame_lambda, shear_modulus)
    adjoint_final = jnp.stack(fields)
    kernel = jnp.sum(fields[2] * forward_field, axis=0)
    slot_rows = jnp.dot(patch_basis, kernel, precision=precise_mode)
    n_slots = patch_ids.shape[1]
    n_patch = owner_map.shape[0]
    slot_used = lax.iota(jnp.int32, n_slots) < slot_counts[0]
    slot_ids = patch_ids[0]
    patch_order = lax.iota(jnp.int32, n_patch)
    same_owner = owner_map[:, None] == owner_map[None, :]
    earlier = patch_order[None, :] < patch_order[:, None]
    patch_rank = jnp.sum((same_owner & earlier).astype(jnp.int32), axis=1)
    rank_slots = lax.iota(jnp.int32, OWN_CAP)
    target = owner_map[slot_ids]
    dest_hot = (
        (target[:, None] == lax.iota(jnp.int32, tile_count)[None, :]) & slot_used[:, None]
    ).astype(jnp.int32)
    running = jnp.cumsum(dest_hot, axis=0) - 1
    position = jnp.sum(dest_hot * running, axis=1)
    buffer_index = target * CAP + position
    selector = (
        lax.iota(jnp.int32, tile_count * CAP)[:, None] == buffer_index[None, :]
    ) & slot_used[None, :]
    send_rows = jnp.dot(selector.astype(jnp.float32), slot_rows, precision=precise_mode).reshape(
        tile_count, CAP, y_cells
    )
    send_ids = jnp.sum(jnp.where(selector, slot_ids[None, :], 0), axis=1).reshape(tile_count, CAP)
    got_rows, got_ids = (
        lax.all_to_all(send_rows, "horiz", split_axis=0, concat_axis=0, tiled=True),
        lax.all_to_all(send_ids, "horiz", split_axis=0, concat_axis=0, tiled=True),
    )
    got_rows = got_rows.reshape(tile_count * CAP, y_cells)
    got_ids = got_ids.reshape(tile_count * CAP)
    placing = (
        (patch_rank[got_ids][None, :] == rank_slots[:, None])
        & (owner_map[got_ids] == tile_index)[None, :]
    ).astype(jnp.float32)
    patch_grad = jnp.dot(placing, got_rows, precision=precise_mode)
    return (adjoint_final, cross[None], patch_grad[None])


LEV, XC, YC, STN, BLK, FREQ = 8, 16, 128, 32, 8, 8
VX, VY, VZ, SXX, SYY, SZZ, SXY, SXZ, SYZ, BUO, LAM, MU = range(12)
EXT_X = XC + 8
FIRST = 5
CHUNKS = 6
EARLY = 3
WIDE = 2
V_LEVELS = 16
S_LEVELS = 14
ALL_VMEM = 67043328
SPARE = 2**11
MESH = pl.DeviceIdType.MESH


def split3(value):
    high = value.astype(jnp.bfloat16)
    rest = value - high.astype(jnp.float32)
    mid = rest.astype(jnp.bfloat16)
    low = (rest - mid.astype(jnp.float32)).astype(jnp.bfloat16)
    return high, mid, low


def dot32(a, b, dims):
    return lax.dot_general(
        a, b, (dims, ((), ())), precision=precise_mode, preferred_element_type=jnp.float32
    )


def roll_x(f, up):
    return pltpu.roll(f, EXT_X - 1 if up else 1, 0)


def velocity_levels(ext, mats, first, count):
    lane = lax.broadcasted_iota(jnp.int32, (EXT_X, YC), 1)

    def ahead_y(f):
        return jnp.where(lane == YC - 1, 0.0, pltpu.roll(f, YC - 1, 1)) - f

    def behind_y(f):
        return f - jnp.where(lane == 0, 0.0, pltpu.roll(f, 1, 1))

    for i in range(count):
        z = first + i
        sxy = ext[SXY, z]
        sxz = ext[SXZ, z]
        syz = ext[SYZ, z]
        sxx = ext[SXX, z]
        scale = time_step * mats[BUO, z]
        vx = ext[VX, z] + scale * (
            (roll_x(sxx, True) - sxx) + behind_y(sxy) + (sxz - ext[SXZ, z - 1])
        )
        vy = ext[VY, z] + scale * (
            (sxy - roll_x(sxy, False)) + ahead_y(ext[SYY, z]) + (syz - ext[SYZ, z - 1])
        )
        vz = ext[VZ, z] + scale * (
            (sxz - roll_x(sxz, False)) + behind_y(syz) + (ext[SZZ, z + 1] - ext[SZZ, z])
        )
        for k, value in zip((VX, VY, VZ), (vx, vy, vz)):
            ext[k, z] = value


def stress_levels(ext, mats, first, count):
    lane = lax.broadcasted_iota(jnp.int32, (EXT_X, YC), 1)

    def ahead_y(f):
        return jnp.where(lane == YC - 1, 0.0, pltpu.roll(f, YC - 1, 1)) - f

    def behind_y(f):
        return f - jnp.where(lane == 0, 0.0, pltpu.roll(f, 1, 1))

    for i in range(count):
        z = first + i
        vx = ext[VX, z]
        vy = ext[VY, z]
        vz = ext[VZ, z]
        lam = time_step * mats[LAM, z]
        mu = time_step * mats[MU, z]
        exx = vx - roll_x(vx, False)
        eyy = behind_y(vy)
        ezz = vz - ext[VZ, z - 1]
        p_mod = lam + 2.0 * mu
        sxx = ext[SXX, z] + (p_mod * exx + lam * (eyy + ezz))
        syy = ext[SYY, z] + (p_mod * eyy + lam * (exx + ezz))
        szz = ext[SZZ, z] + (p_mod * ezz + lam * (exx + eyy))
        sxy = ext[SXY, z] + mu * (ahead_y(vx) + (roll_x(vy, True) - vy))
        sxz = ext[SXZ, z] + mu * ((ext[VX, z + 1] - vx) + (roll_x(vz, True) - vz))
        syz = ext[SYZ, z] + mu * ((ext[VY, z + 1] - vy) + ahead_y(vz))
        for k, value in zip((SXX, SYY, SZZ, SXY, SXZ, SYZ), (sxx, syy, szz, sxy, sxz, syz)):
            ext[k, z] = value


def in_trips(levels, ext, first, total, count):
    def body(i, carry):
        levels(ext, ext, first + count * i, count)
        return carry

    trips, rest = divmod(total, count)
    if trips:
        lax.fori_loop(0, trips, body, 0)
    if rest:
        levels(ext, ext, first + count * trips, rest)


def fused_kernel(
    tiles,
    slabs,
    state_ref,
    buo_ref,
    lam_ref,
    mu_ref,
    forward_hbm,
    traces_hbm,
    observed_hbm,
    pairs_hbm,
    basis_hbm,
    ids_hbm,
    counts_hbm,
    owner_hbm,
    table_hbm,
    final_out,
    cross_out,
    rows_in,
    ext,
    cross_ref,
    forward_ref,
    traces_ref,
    observed_ref,
    pairs_ref,
    basis_ref,
    ids_ref,
    counts_ref,
    owner_ref,
    table_ref,
    pack_r,
    pack_l,
    halo_r,
    halo_l,
    spec_out,
    spec_in,
    left_rows,
    right_rows,
    part,
    parts,
    added,
    rows_out,
    local_sem,
    spec_send,
    spec_recv,
    slab_send,
    slab_recv,
    side_send,
    side_recv,
    corner_send,
    corner_recv,
    part_send,
    part_recv,
    row_send,
    row_recv,
    far_sem,
):
    me = lax.axis_index("horiz")
    depth = lax.axis_index("depth")
    n_pairs = pairs_ref.shape[1]
    own = pl.ds(FIRST, LEV)
    arrays = ((0, 9, state_ref), (9, 1, buo_ref), (10, 1, lam_ref), (11, 1, mu_ref))
    pair_rows = tiles // WIDE
    row_z, row_y = me // WIDE, lax.rem(me, WIDE)

    barrier = pltpu.get_barrier_semaphore()
    for d in range(1, slabs):
        other = {"depth": lax.rem(depth + d, slabs)}
        pl.semaphore_signal(barrier, inc=1, device_id=other, device_id_type=MESH)
    for k in range(1, WIDE):
        other = {"horiz": row_z * WIDE + lax.rem(row_y + k, WIDE)}
        pl.semaphore_signal(barrier, inc=1, device_id=other, device_id_type=MESH)

    def near_rows(run):
        for step in (-1, 1):

            @pl.when((row_z + step >= 0) & (row_z + step < pair_rows))
            def _():
                run(step)

    def greet(step):
        for k in range(WIDE):
            other = {"horiz": (row_z + step) * WIDE + k}
            pl.semaphore_signal(barrier, inc=1, device_id=other, device_id_type=MESH)

    near_rows(greet)

    smalls = (
        (traces_hbm, traces_ref),
        (table_hbm, table_ref),
        (pairs_hbm, pairs_ref),
        (basis_hbm, basis_ref),
        (ids_hbm, ids_ref),
        (counts_hbm, counts_ref),
        (owner_hbm, owner_ref),
        (observed_hbm, observed_ref),
        (forward_hbm, forward_ref),
    )
    small_in = [
        pltpu.make_async_copy(src, dst, local_sem.at[4 + n]) for n, (src, dst) in enumerate(smalls)
    ]
    locals_in = [
        pltpu.make_async_copy(
            src, ext.at[pl.ds(start, count), own, pl.ds(0, XC)], local_sem.at[n]
        )
        for n, (start, count, src) in enumerate(arrays)
    ]
    for copy in small_in[:2] + locals_in + small_in[2:]:
        copy.start()

    row = lax.broadcasted_iota(jnp.int32, (8, YC), 0)
    lower = row < 4
    for copy in small_in[:2]:
        copy.wait()
    by_block = jnp.concatenate(
        [traces_ref[pl.ds(b, STN, stride=BLK), :] for b in range(BLK)], axis=0
    )
    spectra = dot32(table_ref[...], by_block, ((1,), (1,)))
    half = tiles * FREQ
    for t in range(tiles):
        for c in range(2):
            spec_out[t, pl.ds(c * FREQ, FREQ), :] = spectra[
                c * half + t * FREQ : c * half + (t + 1) * FREQ
            ]
    for copy in locals_in:
        copy.wait()

    def pack_one(a, carry):
        for j in range(LEV // 2):
            even, odd = FIRST + 2 * j, FIRST + 2 * j + 1
            pack_r[a, j] = jnp.where(
                lower, ext[a, even, pl.ds(0, 8)], pltpu.roll(ext[a, odd, pl.ds(0, 8)], 4, 0)
            )
            pack_l[a, j] = jnp.where(
                lower, pltpu.roll(ext[a, odd, pl.ds(8, 8)], 4, 0), ext[a, even, pl.ds(8, 8)]
            )
        return carry

    lax.fori_loop(0, 12, pack_one, 0)

    mid_pairs = pl.ds(2, LEV // 2)

    def side_copy(n, c):
        source, target, step = ((pack_r, halo_r, -1), (pack_l, halo_l, 1))[n]
        some = pl.ds(c * 12 // CHUNKS, 12 // CHUNKS)
        return pltpu.make_async_remote_copy(
            src_ref=source.at[some],
            dst_ref=target.at[some, mid_pairs],
            send_sem=side_send.at[n],
            recv_sem=side_recv.at[n, c],
            device_id={"horiz": me + step},
            device_id_type=MESH,
        )

    def slab_copy(n, m):
        start, count, src = arrays[m]
        levels = pl.ds(0, 4) if n == 0 else pl.ds(LEV - 4, 4)
        source = src.at[:, levels]
        target = ext.at[
            pl.ds(start, count), pl.ds(FIRST + LEV if n == 0 else FIRST - 4, 4), pl.ds(0, XC)
        ]
        return pltpu.make_async_remote_copy(
            src_ref=source,
            dst_ref=target,
            send_sem=slab_send.at[n],
            recv_sem=slab_recv.at[n],
            device_id={"depth": depth + (-1 if n == 0 else 1)},
            device_id_type=MESH,
        )

    def corner_copy(n, m, c):
        buffer = (halo_r, halo_l)[m]
        some = pl.ds(c * 12 // CHUNKS, 12 // CHUNKS)
        return pltpu.make_async_remote_copy(
            src_ref=buffer.at[some, pl.ds(2 if n == 0 else 4, 2)],
            dst_ref=buffer.at[some, pl.ds(6 if n == 0 else 0, 2)],
            send_sem=corner_send.at[n, m],
            recv_sem=corner_recv.at[n, m],
            device_id={"depth": depth + (-1 if n == 0 else 1)},
            device_id_type=MESH,
        )

    def whole(src, dst, send, recv):
        return pltpu.make_async_remote_copy(
            src_ref=src,
            dst_ref=dst,
            send_sem=send,
            recv_sem=recv,
            device_id={"horiz": me},
            device_id_type=MESH,
        )

    def sides(n):
        source, target = ((pack_r, halo_r), (pack_l, halo_l))[n]
        return whole(source, target.at[:, mid_pairs], side_send.at[n], side_recv.at[n, 0])

    def slab(n):
        levels = ext.at[
            :, pl.ds(FIRST + LEV if n == 0 else FIRST - 4, 4), pl.ds(0, XC)
        ]
        return whole(levels, levels, slab_send.at[n], slab_recv.at[n])

    def corners(n, m):
        buffer = (halo_r, halo_l)[m]
        return whole(
            buffer.at[:, pl.ds(2 if n == 0 else 4, 2)],
            buffer.at[:, pl.ds(6 if n == 0 else 0, 2)],
            corner_send.at[n, m],
            corner_recv.at[n, m],
        )

    has_left, has_right = me > 0, me < tiles - 1
    has_up, has_down = depth > 0, depth < slabs - 1

    def side_start(c):
        @pl.when(has_left)
        def _():
            side_copy(0, c).start()

        @pl.when(has_right)
        def _():
            side_copy(1, c).start()

    def spec_copy(peer, source):
        return pltpu.make_async_remote_copy(
            src_ref=spec_out.at[peer],
            dst_ref=spec_in.at[source],
            send_sem=spec_send,
            recv_sem=spec_recv,
            device_id={"horiz": peer},
            device_id_type=MESH,
        )

    def far_signal(step, stage):
        pl.semaphore_signal(
            far_sem.at[(step + 1) // 2, stage],
            inc=1,
            device_id={"horiz": me + step * WIDE},
            device_id_type=MESH,
        )

    def spec_row(distance):
        for step in (-1, 1):
            there = row_z + step * distance

            @pl.when((there >= 0) & (there < pair_rows))
            def _():
                for k in range(WIDE):
                    spec_copy(there * WIDE + k, me).start()

    pl.semaphore_wait(
        barrier,
        slabs
        - 1
        + WIDE
        - 1
        + jnp.where(row_z > 0, WIDE, 0)
        + jnp.where(row_z < pair_rows - 1, WIDE, 0),
    )
    for step in (-1, 1):

        @pl.when(
            (row_z - step >= 0)
            & (row_z - step < pair_rows)
            & (row_z + step >= 0)
            & (row_z + step < pair_rows)
        )
        def _():
            far_signal(step, 0)

    for c in range(EARLY):
        side_start(c)

    @pl.when(has_up)
    def _():
        for m in range(4):
            slab_copy(0, m).start()

    @pl.when(has_down)
    def _():
        for m in range(4):
            slab_copy(1, m).start()

    for k in range(1, WIDE):
        spec_copy(row_z * WIDE + lax.rem(row_y + k, WIDE), me).start()
    spec_row(1)
    for distance in range(2, pair_rows):
        for step in (-1, 1):
            source = row_z - step * distance
            after = row_z + step

            @pl.when((source >= 0) & (source < pair_rows))
            def _():
                pl.semaphore_wait(far_sem.at[(step + 1) // 2, distance - 2], 1)
                if distance < pair_rows - 1:

                    @pl.when((after >= 0) & (after < pair_rows))
                    def _():
                        far_signal(step, distance - 1)

        spec_row(distance)
    for c in range(EARLY, CHUNKS):
        side_start(c)
    spec_in[me] = spec_out[me]

    def clear_levels(first):
        def clear(a, carry):
            for i in range(4):
                ext[a, first + i] = jnp.zeros((EXT_X, YC), jnp.float32)
            return carry

        lax.fori_loop(0, 12, clear, 0)

    def clear_pairs(buffer, first, count):
        def clear(a, carry):
            for i in range(count):
                buffer[a, first + i] = jnp.zeros((8, YC), jnp.float32)
            return carry

        lax.fori_loop(0, 12, clear, 0)

    @pl.when(jnp.logical_not(has_up))
    def _():
        clear_levels(FIRST - 4)
        clear_pairs(halo_r, 0, 2)
        clear_pairs(halo_l, 0, 2)

    @pl.when(jnp.logical_not(has_down))
    def _():
        clear_levels(FIRST + LEV)
        clear_pairs(halo_r, 6, 2)
        clear_pairs(halo_l, 6, 2)

    @pl.when(jnp.logical_not(has_right))
    def _():
        clear_pairs(halo_r, 2, 4)

    @pl.when(jnp.logical_not(has_left))
    def _():
        clear_pairs(halo_l, 2, 4)

    def clear_ends(a, carry):
        ext[a, 0] = jnp.zeros((EXT_X, YC), jnp.float32)
        ext[a, 17] = jnp.zeros((EXT_X, YC), jnp.float32)
        return carry

    lax.fori_loop(0, 12, clear_ends, 0)

    def clear_added(a, carry):
        for i in range(ITERS + 3):
            added[a, FIRST - 1 + i] = jnp.zeros((EXT_X, YC), jnp.float32)
        return carry

    @pl.when(depth == 0)
    def _():
        lax.fori_loop(0, 9, clear_added, 0)

    for copy in small_in[2:7]:
        copy.wait()
    first_pair = pairs_ref[pl.ds(0, 1), :]
    second_pair = pairs_ref[pl.ds(1, 1), :]
    stations = tiles * STN
    station = lax.broadcasted_iota(jnp.int32, (stations, n_pairs), 0)
    hot_first = (station == first_pair).astype(jnp.float32).astype(jnp.bfloat16)
    hot_second = (station == second_pair).astype(jnp.float32).astype(jnp.bfloat16)
    n_patch = owner_ref.shape[1]
    n_slots = ids_ref.shape[1]
    owner_row = owner_ref[...]
    up_iota = lax.broadcasted_iota(jnp.int32, (n_patch, n_patch), 0)
    across = lax.broadcasted_iota(jnp.int32, (n_patch, n_patch), 1)
    owner_wide = jnp.broadcast_to(owner_row, (n_patch, n_patch))
    owner_col = jnp.sum(jnp.where(up_iota == across, owner_wide, 0), axis=1, keepdims=True)
    rank_row = jnp.sum(
        jnp.where((owner_col == owner_wide) & (up_iota < across), 1, 0), axis=0, keepdims=True
    )
    target_row = owner_row * OWN_CAP + rank_row
    out_rows = tiles * OWN_CAP
    place = (
        lax.broadcasted_iota(jnp.int32, (out_rows, n_patch), 0) == target_row
    ).astype(jnp.float32)
    slot = lax.broadcasted_iota(jnp.int32, (n_patch, n_slots), 1)
    patch = lax.broadcasted_iota(jnp.int32, (n_patch, n_slots), 0)
    named = ((patch == ids_ref[...]) & (slot < counts_ref[...])).astype(jnp.float32)
    slot_place = dot32(place, named, ((1,), (0,)))
    row_basis = dot32(slot_place, basis_ref[...], ((1,), (0,)))

    def relay(first, last):
        for c in range(first, last):

            @pl.when(has_left)
            def _():
                side_copy(1, c).wait_recv()

            @pl.when(has_right)
            def _():
                side_copy(0, c).wait_recv()

            @pl.when(has_up)
            def _():
                for m in range(2):
                    corner_copy(0, m, c).start()

            @pl.when(has_down)
            def _():
                for m in range(2):
                    corner_copy(1, m, c).start()

    relay(0, EARLY)
    others = pl.ds(0, tiles - 1)
    whole(spec_out.at[others], spec_in.at[others], spec_send, spec_recv).wait_recv()
    small_in[7].wait()
    for b in range(BLK):
        wide = jnp.concatenate(
            [spec_in[t][:, b * STN : (b + 1) * STN] for t in range(tiles)], axis=1
        )
        left_rows[pl.ds(b * 2 * FREQ, 2 * FREQ), :] = wide[:, :128]
        right_rows[pl.ds(b * 2 * FREQ, 2 * FREQ), :] = wide[:, 128:]
    ordered = jnp.concatenate(
        [
            jnp.concatenate(
                [r[pl.ds(cf, BLK, stride=2 * FREQ), :] for cf in range(2 * FREQ)], axis=0
            )
            for r in (left_rows, right_rows)
        ],
        axis=1,
    )
    pieces = split3(ordered)

    def gather(hot):
        return sum(
            lax.dot_general(
                piece, hot, (((1,), (0,)), ((), ())), preferred_element_type=jnp.float32
            )
            for piece in pieces[::-1]
        )

    first_spec = gather(hot_first)
    second_spec = gather(hot_second)
    items = FREQ * BLK
    f_re, f_im = first_spec[:items], first_spec[items:]
    s_re, s_im = second_spec[:items], second_spec[items:]
    cross_re = f_re * s_re + f_im * s_im
    cross_im = f_re * s_im - f_im * s_re
    items_all = items * tiles * slabs
    item = lax.broadcasted_iota(jnp.int32, (items, 1), 0) + (depth * tiles + me) * items
    weight = 1.0 + 2.0 * item.astype(jnp.float32) / (items_all - 1)
    dev_re = cross_re - observed_ref[0, 0]
    dev_im = cross_im - observed_ref[0, 1]
    terms = weight * (dev_re * dev_re + dev_im * dev_im)
    part[...] = jnp.sum(terms, axis=0, keepdims=True)

    def part_copy(d, k):
        slot = d * tiles + me
        return pltpu.make_async_remote_copy(
            src_ref=part,
            dst_ref=parts.at[slot],
            send_sem=part_send,
            recv_sem=part_recv,
            device_id={"horiz": lax.rem(me + k, tiles), "depth": 0},
            device_id_type=MESH,
        )

    for k in range(1, tiles):
        part_copy(depth, k).start()

    @pl.when(depth > 0)
    def _():
        part_copy(depth, 0).start()

    cross_ref[0, 0] = cross_re
    cross_ref[0, 1] = cross_im
    cross_copy = pltpu.make_async_copy(cross_ref, cross_out, local_sem.at[13])
    cross_copy.start()

    relay(EARLY, CHUNKS)

    def unpack(first, count):
        def unpack_one(a, carry):
            for j in range(first, first + count):
                r, l = halo_r[a, j], halo_l[a, j]
                ext[a, 1 + 2 * j, pl.ds(XC, 8)] = jnp.where(lower, r, l)
                ext[a, 2 + 2 * j, pl.ds(XC, 8)] = pltpu.roll(jnp.where(lower, l, r), 4, 0)
            return carry

        lax.fori_loop(0, 12, unpack_one, 0)

    unpack(2, 4)

    @pl.when(has_up)
    def _():
        slab(1).wait_recv()
        for m in range(2):
            corners(1, m).wait_recv()

    @pl.when(has_down)
    def _():
        slab(0).wait_recv()
        for m in range(2):
            corners(0, m).wait_recv()

    unpack(0, 2)
    unpack(6, 2)

    for n in range(ITERS):
        in_trips(velocity_levels, ext, 1 + n, 16 - 2 * n, V_LEVELS)
        in_trips(stress_levels, ext, 2 + n, 14 - 2 * n, S_LEVELS)

    @pl.when(depth == 0)
    def _():
        senders = parts.at[pl.ds(0, tiles * slabs - 1)]
        whole(senders, senders, part_send, part_recv).wait_recv()
        parts[me] = part[...]
        total = parts[0]
        for t in range(1, tiles * slabs):
            total = total + parts[t]
        terms = total / (2.0 * items_all)
        ext_row = lax.broadcasted_iota(jnp.int32, (EXT_X, 1), 0)
        x = me * XC + jnp.where(ext_row < XC + 4, ext_row, ext_row - EXT_X)
        x_pos = x + XC
        tile = x_pos // XC - 1
        in_tile = x_pos - (tile + 1) * XC
        lane = lax.broadcasted_iota(jnp.int32, (EXT_X, YC), 1)
        deposit = jnp.zeros((EXT_X, YC), jnp.float32)
        for turn in range(STN // XC):
            within = in_tile + turn * XC
            index = tile * STN + within
            hits = (index == first_pair).astype(jnp.float32) + (index == second_pair).astype(
                jnp.float32
            )
            sums = jnp.sum(hits * terms, axis=1, keepdims=True)
            number = jnp.sum(hits, axis=1, keepdims=True)
            value = sums / jnp.maximum(number, 1.0)
            deposit = deposit + jnp.where(lane == lax.rem(53 * within, YC), value, 0.0)
        added[VZ, FIRST] = deposit
        for n in range(ITERS):
            if n:
                velocity_levels(added, ext, FIRST, n + 1)
            stress_levels(added, ext, FIRST, n + 2)

        def add_one(a, carry):
            for i in range(ITERS + 1):
                ext[a, FIRST + i, pl.ds(0, XC)] += added[a, FIRST + i, pl.ds(0, XC)]
            return carry

        lax.fori_loop(0, 9, add_one, 0)

    final = pltpu.make_async_copy(
        ext.at[pl.ds(0, 9), own, pl.ds(0, XC)], final_out, local_sem.at[14]
    )
    final.start()
    small_in[8].wait()
    weighted = sum(ext[VZ, FIRST + i, pl.ds(0, XC)] * forward_ref[i] for i in range(LEV))
    rows = dot32(row_basis, weighted, ((1,), (0,)))
    for t in range(tiles):
        rows_out[t] = rows[t * OWN_CAP : (t + 1) * OWN_CAP]
    row_copies = []
    for k in range(1, tiles):
        peer = lax.rem(me + k, tiles)
        row_copies.append(
            pltpu.make_async_remote_copy(
                src_ref=rows_out.at[peer],
                dst_ref=rows_in.at[me],
                send_sem=row_send,
                recv_sem=row_recv,
                device_id={"horiz": peer},
                device_id_type=MESH,
            )
        )
    for copy in row_copies:
        copy.start()
    own_rows = pltpu.make_async_copy(rows_out.at[me], rows_in.at[me], local_sem.at[15])
    own_rows.start()

    whole(spec_out.at[others], spec_in.at[others], spec_send, spec_recv).wait_send()

    @pl.when(has_left)
    def _():
        sides(0).wait_send()

    @pl.when(has_right)
    def _():
        sides(1).wait_send()

    @pl.when(has_up)
    def _():
        slab(0).wait_send()
        for m in range(2):
            corners(0, m).wait_send()

    @pl.when(has_down)
    def _():
        slab(1).wait_send()
        for m in range(2):
            corners(1, m).wait_send()

    @pl.when(depth == 0)
    def _():
        sent = parts.at[pl.ds(0, tiles - 1)]
        whole(sent, sent, part_send, part_recv).wait_send()

    @pl.when(depth > 0)
    def _():
        sent = parts.at[pl.ds(0, tiles)]
        whole(sent, sent, part_send, part_recv).wait_send()

    all_rows = whole(rows_out.at[others], rows_in.at[others], row_send, row_recv)
    all_rows.wait_recv()
    all_rows.wait_send()
    own_rows.wait()
    cross_copy.wait()
    final.wait()


def hand_out_kernel(state, cross, rows, state_ref, cross_ref, grad_ref, grad, out_sem):
    writes = [
        pltpu.make_async_copy(src, dst, out_sem.at[n])
        for n, (src, dst) in enumerate(
            ((state, state_ref), (cross, cross_ref), (grad, grad_ref))
        )
    ]
    writes[0].start()
    writes[1].start()
    grad[0] = sum(rows[t] for t in range(rows.shape[0]))
    writes[2].start()
    for write in writes:
        write.wait()


def hand_out(state, cross, rows):
    anywhere = pl.BlockSpec(memory_space=pl.ANY)
    vmem = pl.BlockSpec(memory_space=pltpu.VMEM)
    grad = jax.ShapeDtypeStruct((1,) + rows.shape[1:], rows.dtype)
    return pl.pallas_call(
        hand_out_kernel,
        out_shape=(
            jax.ShapeDtypeStruct(state.shape, state.dtype),
            jax.ShapeDtypeStruct(cross.shape, cross.dtype),
            grad,
        ),
        in_specs=[anywhere, anywhere, vmem],
        out_specs=(anywhere,) * 3,
        scratch_shapes=[
            pltpu.VMEM(grad.shape, grad.dtype),
            pltpu.SemaphoreType.DMA((3,)),
        ],
        compiler_params=pltpu.CompilerParams(vmem_limit_bytes=2**20),
    )(state, cross, rows)


def fused_shards(
    adjoint_state,
    buoyancy,
    lame_lambda,
    shear_modulus,
    forward_field,
    traces,
    observed,
    pairs,
    patch_basis,
    patch_ids,
    slot_counts,
    owner_map,
):
    tiles, slabs = lax.axis_size("horiz"), lax.axis_size("depth")
    samples = traces.shape[2]
    n_pairs = pairs.shape[0]
    bins = samples // 2
    phases = np.outer(np.arange(1, bins + 1), np.arange(samples)) % samples
    angles = phases * (2.0 * math.pi / samples)
    table = np.concatenate([np.cos(angles), -np.sin(angles)], axis=0) / math.sqrt(samples)
    anywhere = pl.BlockSpec(memory_space=pl.ANY)
    f32 = jnp.float32
    dma = pltpu.SemaphoreType.DMA
    kept = 4 * (
        math.prod(adjoint_state.shape) + math.prod(observed.shape) + tiles * OWN_CAP * YC
    )
    return pl.pallas_call(
        functools.partial(fused_kernel, tiles, slabs),
        out_shape=(
            pltpu.VMEM(adjoint_state.shape, f32),
            pltpu.VMEM(observed.shape, f32),
            pltpu.VMEM((tiles, OWN_CAP, YC), f32),
        ),
        in_specs=[anywhere] * 13,
        out_specs=(anywhere, anywhere, anywhere),
        scratch_shapes=[
            pltpu.VMEM((12, LEV + 10, EXT_X, YC), f32),
            pltpu.VMEM(observed.shape, f32),
            pltpu.VMEM(forward_field.shape, f32),
            pltpu.VMEM((STN * BLK, samples), f32),
            pltpu.VMEM(observed.shape, f32),
            pltpu.VMEM((2, n_pairs), jnp.int32),
            pltpu.VMEM(patch_basis.shape, f32),
            pltpu.VMEM(patch_ids.shape, jnp.int32),
            pltpu.VMEM((1, 1), jnp.int32),
            pltpu.VMEM((1, owner_map.shape[0]), jnp.int32),
            pltpu.VMEM(table.shape, f32),
            pltpu.VMEM((12, 4, 8, YC), f32),
            pltpu.VMEM((12, 4, 8, YC), f32),
            pltpu.VMEM((12, 8, 8, YC), f32),
            pltpu.VMEM((12, 8, 8, YC), f32),
            pltpu.VMEM((tiles, 2 * FREQ, BLK * STN), f32),
            pltpu.VMEM((tiles, 2 * FREQ, BLK * STN), f32),
            pltpu.VMEM((2 * FREQ * BLK, 128), f32),
            pltpu.VMEM((2 * FREQ * BLK, 128), f32),
            pltpu.VMEM((1, n_pairs), f32),
            pltpu.VMEM((tiles * slabs, 1, n_pairs), f32),
            pltpu.VMEM((9, FIRST + ITERS + 2, EXT_X, YC), f32),
            pltpu.VMEM((tiles, OWN_CAP, YC), f32),
            dma((16,)),
            pltpu.SemaphoreType.DMA(()),
            pltpu.SemaphoreType.DMA(()),
            dma((2,)),
            dma((2,)),
            dma((2,)),
            dma((2, CHUNKS)),
            dma((2, 2)),
            dma((2, 2)),
            pltpu.SemaphoreType.DMA(()),
            pltpu.SemaphoreType.DMA(()),
            pltpu.SemaphoreType.DMA(()),
            pltpu.SemaphoreType.DMA(()),
            pltpu.SemaphoreType.REGULAR((2, max(tiles // WIDE - 2, 1))),
        ],
        compiler_params=pltpu.CompilerParams(
            collective_id=0, has_side_effects=True, vmem_limit_bytes=ALL_VMEM - kept - SPARE
        ),
    )(
        adjoint_state,
        buoyancy[None],
        lame_lambda[None],
        shear_modulus[None],
        forward_field,
        traces.reshape(-1, samples),
        observed,
        pairs.T,
        patch_basis,
        patch_ids,
        slot_counts.reshape(1, 1),
        owner_map.reshape(1, -1),
        jnp.asarray(table, f32),
    )


def fits_fused(tiles, slabs, state, traces, pairs):
    return (
        state[1:] == (LEV, XC, YC)
        and traces == (STN, BLK, 128)
        and tiles * FREQ == 64
        and slabs > 1
        and pairs[0] % 128 == 0
    )


def local_program(*args):
    tiles, slabs = lax.axis_size("horiz"), lax.axis_size("depth")
    if fits_fused(tiles, slabs, args[0].shape, args[5].shape, args[7].shape):
        return hand_out(*fused_shards(*args))
    return shards(*args)


def solution(mesh):
    return jax.shard_map(
        local_program,
        mesh=mesh,
        in_specs=(
            P(None, "depth", "horiz", None),
            P("depth", "horiz", None),
            P("depth", "horiz", None),
            P("depth", "horiz", None),
            P("depth", "horiz", None),
            P("horiz", "depth", None),
            P("depth", None, "horiz", None),
            P(),
            P(None, "horiz"),
            P("horiz", None),
            P("horiz"),
            P(),
        ),
        out_specs=(
            P(None, "depth", "horiz", None),
            P("depth", None, "horiz", None),
            P("depth", "horiz", None),
        ),
        check_vma=False,
    )
```
